32 devices in a mesh: band: 32 (over z, y, x, core).
Axes of the slice: x: 2, y: 2, z: 4, core: 2. Of those that a mesh axis runs over, the one named last changes fastest.
Arguments:
- rho_low: float32 [2, 32, 128, 128], replicated, may hold values from -6 to 6
- kprev_low: float32 [2, 32, 128, 128], replicated, may hold values from -6 to 6
- rho_band: float32 [2, 512, 128, 128], P(None, 'band'), may hold values from -6 to 6
- kprev_band: float32 [2, 512, 128, 128], P(None, 'band'), may hold values from -6 to 6
- hamiltonian: float32 [2, 128, 128], replicated, as said below
- state_site: int32 [128], replicated, may hold values from 0 to 23
- coupling_mag: float32 [72], replicated, may hold values from 0.2 to 2
- coupling_phase: float32 [72], replicated, may hold values from -3.140625 to 3.140625
- damping_rate: float32 [72], replicated, may hold values from 0.05 to 2
- low_mode: int32 [31], replicated, may hold values from 0 to 71, as said below
- occupation: int32 [512, 72], P('band'), may hold values from 0 to 3, as said below
- couple_src: int32 [512, 16], P('band'), may hold values from -1 to 543, as said below
- couple_mode: int32 [512, 16], P('band'), may hold values from 0 to 71, as said below
- couple_dir: int32 [512, 16], P('band'), may hold values from 0 to 1
Outputs:
- k_low: float32 [2, 32, 128, 128], replicated
- k_band: float32 [2, 512, 128, 128], P(None, 'band')
The draws below stay inside these ranges and needn't reach their ends.
Inputs may be any that keep to these rules, and one draw needn't show every extreme that they name: `hamiltonian`: the real part is symmetric and the imaginary part antisymmetric (a Hermitian matrix). `low_mode`: distinct modes. `occupation`: each operator has one to three quanta in all. `couple_src`: all couplings of one device's operators to operators held by one other device read one and the same operator of that device. A low-tier source is never 0, and couplings to low-tier sources have direction 1. Each device's far couplings reach devices spread over the whole axis. `couple_mode`: for direction 1 the mode is occupied in the destination operator.
All inputs are finite; a program needn't handle non-finite values.
Results may differ from the reference program's by a relative error of at most 0.0003.
Values sent between devices are 32-bit elements; how exact they have to be, the bound alone decides.
No kernel may reach another device: no remote copies, remote signals or barrier semaphores. Data moves between devices by JAX's collectives and lax.ppermute only.
A program may use at most 192 MiB of HBM per device.

```python
import math
import jax
import jax.numpy as jnp
from jax import lax

S = 128
SITES = 24
EXPS = 3
MODES = 72
LOW = 32
ADO_DEV = 16
DEG = 16
FAR_DEG = 8
BAND_TOTAL = 512
N_BAND = 32


def hierarchy_plan(key):
    base = jax.random.fold_in(key, 7001)
    keys = jax.random.split(base, 9)
    band_size = N_BAND
    glob = jnp.arange(BAND_TOTAL)
    device = glob // ADO_DEV
    within = glob % ADO_DEV
    raw_picks = jax.random.randint(keys[0], (BAND_TOTAL, 3), 0, MODES)
    stacked = (within == 0)[:, None]
    picks = jnp.where(stacked, raw_picks[:, 0:1], raw_picks)
    mode_ids = jnp.arange(MODES)
    occupation = jnp.sum((picks[:, :, None] == mode_ids[None, None, :]).astype(jnp.int32), axis=1)
    wanted = jax.random.randint(keys[1], (band_size, band_size), 0, ADO_DEV)
    order = within[:, None] * FAR_DEG + jnp.arange(FAR_DEG)[None, :]
    rank_count = min(ADO_DEV * FAR_DEG, band_size - 1)
    rank = order % (band_size - 1)
    spread_off = 2 + (rank - 3) * (band_size - 3) // max(rank_count - 3, 1)
    offset = jnp.where(rank == 0, 1, jnp.where(rank == 1, band_size - 1, jnp.where(rank == 2, band_size // 2, spread_off)))
    peer_dev = (device[:, None] + offset) % band_size
    far_src = LOW + peer_dev * ADO_DEV + wanted[device[:, None], peer_dev]
    rest_cols = DEG - FAR_DEG
    kind = jax.random.randint(keys[2], (BAND_TOTAL, rest_cols), 0, 2)
    low_src = jax.random.randint(keys[3], (BAND_TOTAL, rest_cols), 1, LOW)
    own_src = LOW + device[:, None] * ADO_DEV + jax.random.randint(keys[4], (BAND_TOTAL, rest_cols), 0, ADO_DEV)
    keep = jax.random.randint(keys[5], (BAND_TOTAL, rest_cols), 0, 8) != 0
    near_src = jnp.where(keep, jnp.where(kind == 0, low_src, own_src), -1)
    source = jnp.concatenate([far_src, near_src], axis=1).astype(jnp.int32)
    is_low = jnp.concatenate([jnp.zeros((BAND_TOTAL, FAR_DEG), bool), keep & (kind == 0)], axis=1)
    direction = jnp.where(is_low, 1, jax.random.randint(keys[6], (BAND_TOTAL, DEG), 0, 2)).astype(jnp.int32)
    held = jnp.take_along_axis(picks, jax.random.randint(keys[7], (BAND_TOTAL, DEG), 0, 3), axis=1)
    free_mode = jax.random.randint(keys[8], (BAND_TOTAL, DEG), 0, MODES)
    mode = jnp.where(direction == 1, held, free_mode).astype(jnp.int32)
    return (occupation.astype(jnp.int32), source, mode, direction)


def draw_hamiltonian(key, part):
    first, second, third = jax.random.split(jax.random.fold_in(key, 7003), 3)
    spread = 1.0
    real_raw = jax.random.normal(first, (S, S), jnp.float32) * (0.7 / S ** 0.5)
    imag_raw = jax.random.normal(second, (S, S), jnp.float32) * (0.7 / S ** 0.5)
    energy = jax.random.uniform(third, (S,), jnp.float32, -spread, spread)
    real_part = 0.5 * (real_raw + real_raw.T) + jnp.diag(energy)
    imag_part = 0.5 * (imag_raw - imag_raw.T)
    return jnp.stack([real_part, imag_part]).astype(jnp.float32)


def draw_low_mode(key, part):
    return jax.random.permutation(jax.random.fold_in(key, 7005), MODES)[:LOW - 1].astype(jnp.int32)


def draw_occupation(key, part):
    return hierarchy_plan(key)[0]


def draw_couple_src(key, part):
    return hierarchy_plan(key)[1]


def draw_couple_mode(key, part):
    return hierarchy_plan(key)[2]


def draw_couple_dir(key, part):
    return hierarchy_plan(key)[3]


def place_ends(entries, stream_key, least, largest):
    shape = entries.shape
    place = [jax.random.randint(jax.random.fold_in(stream_key, axis), (), 0, shape[axis]) for axis in range(len(shape))]
    entries = entries.at[tuple(place)].set(least)
    longest = shape.index(max(shape))
    place[longest] = (place[longest] + 1) % shape[longest]
    return entries.at[tuple(place)].set(largest)


def shard_levels(stream_key, shape, cuts, smallest, top_value):
    level = 1.0
    for axis_at, parts in cuts:
        steps = jax.random.uniform(jax.random.fold_in(jax.random.fold_in(stream_key, 6), axis_at), (parts,), jnp.float32, smallest / len(cuts), top_value / len(cuts))
        level = level * jnp.repeat(jnp.exp(steps), shape[axis_at] // parts).reshape((-1,) + (1,) * (len(shape) - 1 - axis_at))
    return level


def scatter_about(rng, dims, scale, most, cuts=(), kind=jnp.bfloat16):
    factor_of = shard_levels(rng, dims, cuts, -0.22, 0.18) if cuts else 1.0
    values = jax.random.normal(rng, dims, jnp.float32) * scale * factor_of
    return jnp.minimum(jnp.maximum(values, -most), most).astype(kind)


def setup_inputs(seed: int = 0) -> dict:
    arg_keys = jax.random.split(jax.random.key(seed), 15)
    rho_low = scatter_about(arg_keys[0], (2, LOW, S, S), 1.0, 6.0, (), jnp.float32)
    kprev_low = scatter_about(arg_keys[1], (2, LOW, S, S), 1.0, 6.0, (), jnp.float32)
    rho_band = scatter_about(arg_keys[2], (2, BAND_TOTAL, S, S), 1.0, 6.0, ((1, 32),), jnp.float32)
    kprev_band = scatter_about(arg_keys[3], (2, BAND_TOTAL, S, S), 1.0, 6.0, ((1, 32),), jnp.float32)
    hamiltonian = draw_hamiltonian(jax.random.fold_in(arg_keys[14], 71), 0)
    state_site = place_ends(jax.random.randint(arg_keys[5], (S,), 0, SITES), jax.random.fold_in(arg_keys[5], 1), 0, SITES - 1).astype(jnp.int32)
    coupling_mag = jnp.clip(jnp.exp(jax.random.uniform(arg_keys[6], (MODES,), jnp.float32, math.log(0.2), math.log(2.0))), 0.2, 2.0)
    coupling_phase = jnp.clip(jax.random.uniform(arg_keys[7], (MODES,), jnp.float32, -3.140625, 3.140625), -3.140625, 3.140625)
    damping_rate = jnp.clip(jnp.exp(jax.random.uniform(arg_keys[8], (MODES,), jnp.float32, math.log(0.05), math.log(2.0))), 0.05, 2.0)
    low_mode = draw_low_mode(jax.random.fold_in(arg_keys[14], 71), 0)
    occupation = draw_occupation(jax.random.fold_in(arg_keys[14], 71), 0)
    couple_src = draw_couple_src(jax.random.fold_in(arg_keys[14], 71), 0)
    couple_mode = draw_couple_mode(jax.random.fold_in(arg_keys[14], 71), 0)
    couple_dir = draw_couple_dir(jax.random.fold_in(arg_keys[14], 71), 0)
    return {"rho_low": rho_low, "kprev_low": kprev_low, "rho_band": rho_band, "kprev_band": kprev_band, "hamiltonian": hamiltonian, "state_site": state_site, "coupling_mag": coupling_mag, "coupling_phase": coupling_phase, "damping_rate": damping_rate, "low_mode": low_mode, "occupation": occupation, "couple_src": couple_src, "couple_mode": couple_mode, "couple_dir": couple_dir}


section_weight = 0.2
highest = lax.Precision.HIGHEST

def commutator(ham, field):
    h_real, h_imag = (ham[0], ham[1])
    y_real, y_imag = (field[0], field[1])

    def left_mul(matrix, block):
        return jnp.einsum('ac,jcb->jab', matrix, block, precision=highest)

    def right_mul(block, matrix):
        return jnp.einsum('jac,cb->jab', block, matrix, precision=highest)
    comm_real = left_mul(h_real, y_real) - left_mul(h_imag, y_imag) - right_mul(y_real, h_real) + right_mul(y_imag, h_imag)
    comm_imag = left_mul(h_real, y_imag) + left_mul(h_imag, y_real) - right_mul(y_real, h_imag) - right_mul(y_imag, h_real)
    return jnp.stack([comm_imag, -comm_real])

def couple_term(source, site_rows, alpha_col, beta_col):
    diff_mask = site_rows[:, :, None] - site_rows[:, None, :]
    sum_mask = site_rows[:, :, None] + site_rows[:, None, :]
    real_part = alpha_col[:, None, None] * diff_mask
    imag_part = beta_col[:, None, None] * sum_mask
    x_real = real_part * source[0] - imag_part * source[1]
    x_imag = real_part * source[1] + imag_part * source[0]
    return jnp.stack([x_imag, -x_real])

def site_masks(state_site, modes):
    owner_site = jnp.arange(modes, dtype=jnp.int32) // EXPS
    return (state_site[None, :] == owner_site[:, None]).astype(jnp.float32)

def low_rest(y_low, site_mask, coupling_mag, coupling_phase, damping_rate, low_mode):
    others = y_low.shape[1] - 1
    site_rows = site_mask[low_mode]
    strength = jnp.sqrt(coupling_mag[low_mode])
    phase_col = coupling_phase[low_mode]
    upward = couple_term(y_low[:, 1:], site_rows, strength, jnp.zeros_like(strength))
    top_term = lax.optimization_barrier(jnp.sum(upward, axis=1, keepdims=True))
    ground = jnp.broadcast_to(y_low[:, 0:1], (2, others) + y_low.shape[2:])
    downward = couple_term(ground, site_rows, strength * jnp.cos(phase_col), strength * jnp.sin(phase_col))
    damping = jnp.concatenate([jnp.zeros((1,), jnp.float32), damping_rate[low_mode]])
    return jnp.concatenate([top_term, downward], axis=1) - damping[None, :, None, None] * y_low

def band_block(y_blk, position, source, mode, direction, occupation, source_pool, ham, site_mask, coupling_mag, coupling_phase, damping_rate, low_mode, low_partial):
    low_count = low_partial.shape[1]
    occ_float = occupation.astype(jnp.float32)
    damping = jnp.dot(occ_float, damping_rate, precision=highest)
    total = commutator(ham, y_blk) - damping[None, :, None, None] * y_blk
    low_marks = jnp.concatenate([jnp.full((1,), -1, jnp.int32), low_mode.astype(jnp.int32)])

    def column(col_id, state_pair):
        total, low_partial = state_pair
        source_col = source[:, col_id]
        mode_col = mode[:, col_id]
        is_down = direction[:, col_id] == 1
        is_live = (source_col >= 0).astype(jnp.float32)
        occ_level = jnp.take_along_axis(occ_float, mode_col[:, None], axis=1)[:, 0]
        strength = coupling_mag[mode_col]
        phase_col = coupling_phase[mode_col]
        amp_up = jnp.sqrt((occ_level + 1.0) * strength)
        amp_down = jnp.sqrt(occ_level * strength)
        alpha_col = jnp.where(is_down, amp_down * jnp.cos(phase_col), amp_up) * is_live
        beta_col = jnp.where(is_down, amp_down * jnp.sin(phase_col), 0.0) * is_live
        site_rows = site_mask[mode_col]
        fetched = jnp.take(source_pool, position[:, col_id], axis=1)
        total = total + couple_term(fetched, site_rows, alpha_col, beta_col)
        is_low = ((source_col >= 0) & (source_col < low_count)).astype(jnp.float32)
        target = jnp.clip(source_col, 0, low_count - 1)
        held_mode = (low_marks[target] == mode_col).astype(jnp.float32)
        alpha_low = jnp.sqrt((held_mode + 1.0) * strength) * is_low
        back_term = couple_term(y_blk, site_rows, alpha_low, jnp.zeros_like(alpha_low))
        low_partial = low_partial.at[:, target].add(back_term)
        return (total, low_partial)
    return lax.fori_loop(0, source.shape[1], column, (total, low_partial))

def reference(rho_low, kprev_low, rho_band, kprev_band, hamiltonian, state_site, coupling_mag, coupling_phase, damping_rate, low_mode, occupation, couple_src, couple_mode, couple_dir):
    y_low = rho_low + section_weight * kprev_low
    y_band = rho_band + section_weight * kprev_band
    site_mask = site_masks(state_site, coupling_mag.shape[0])
    source_pool = jnp.concatenate([y_low, y_band], axis=1)
    block_total = BAND_TOTAL // ADO_DEV

    def block_step(low_partial, block_id):
        row_start = block_id * ADO_DEV
        y_blk = lax.dynamic_slice_in_dim(y_band, row_start, ADO_DEV, 1)
        src_block = lax.dynamic_slice_in_dim(couple_src, row_start, ADO_DEV, 0)
        mode_block = lax.dynamic_slice_in_dim(couple_mode, row_start, ADO_DEV, 0)
        dir_block = lax.dynamic_slice_in_dim(couple_dir, row_start, ADO_DEV, 0)
        occ_block = lax.dynamic_slice_in_dim(occupation, row_start, ADO_DEV, 0)
        position = jnp.maximum(src_block, 0)
        derived, low_partial = band_block(y_blk, position, src_block, mode_block, dir_block, occ_block, source_pool, hamiltonian, site_mask, coupling_mag, coupling_phase, damping_rate, low_mode, low_partial)
        return (low_partial, derived)
    start_partial = jnp.zeros(y_low.shape, jnp.float32)
    low_partial, block_outs = lax.scan(block_step, start_partial, jnp.arange(block_total, dtype=jnp.int32))
    k_band = jnp.moveaxis(block_outs, 0, 1).reshape(y_band.shape)
    k_low = commutator(hamiltonian, y_low) + low_rest(y_low, site_mask, coupling_mag, coupling_phase, damping_rate, low_mode) + low_partial
    return (k_low, k_band)
```

```python
import functools

import jax
import jax.numpy as jnp
from jax import lax
from jax.experimental import pallas as pl
from jax.experimental.pallas import tpu as pltpu
from jax.sharding import PartitionSpec as P

EXPS = 3
section_weight = 0.2
highest = lax.Precision.HIGHEST
VMEM_LIMIT = 60 * 1024 * 1024

vmem = pl.BlockSpec(memory_space=pltpu.VMEM)
smem = pl.BlockSpec(memory_space=pltpu.SMEM)
hbm = pl.BlockSpec(memory_space=pl.ANY)


def fill_masks(col_ref, row_ref, diff_ref, sum_ref):
    sites, size = diff_ref.shape[0], diff_ref.shape[1]

    def one_site(s, carry):
        va = jnp.where(col_ref[...] == s, 1.0, 0.0)
        vb = jnp.where(row_ref[...] == s, 1.0, 0.0)
        va = jnp.broadcast_to(va, (size, size))
        vb = jnp.broadcast_to(vb, (size, size))
        diff_ref[s] = va - vb
        if sum_ref is not None:
            sum_ref[s] = va + vb
        return carry

    lax.fori_loop(0, sites, one_site, 0)


def commutator(left, right, y_pair):
    size = y_pair.shape[-1]
    lhs = jnp.dot(
        left,
        y_pair.reshape(2 * size, size),
        precision=highest,
        preferred_element_type=jnp.float32,
    )
    rhs = jnp.dot(
        jnp.concatenate([y_pair[0], y_pair[1]], axis=1),
        right,
        precision=highest,
        preferred_element_type=jnp.float32,
    )
    return lhs[:size] - rhs[:, :size], lhs[size:] - rhs[:, size:]


def send_kernel(asked, rho, kprev, y_out, send, sems):
    count = rho.shape[1]
    peers = send.shape[0]

    def advance(i, carry):
        for part in range(2):
            y_out[i, part] = rho[part, i] + section_weight * kprev[part, i]
        return carry

    lax.fori_loop(0, count, advance, 0)

    def start(i, carry):
        pltpu.make_async_copy(y_out.at[asked[i]], send.at[i], sems.at[i]).start()
        return carry

    def finish(i, carry):
        pltpu.make_async_copy(y_out.at[0], send.at[i], sems.at[i]).wait()
        return carry

    lax.fori_loop(0, peers, start, 0)
    lax.fori_loop(0, peers, finish, 0)


def low_kernel(
    own_op,
    own_int,
    own_flt,
    count,
    target,
    site,
    alpha,
    y_band,
    rho_own,
    kprev_own,
    rho_top,
    kprev_top,
    left,
    right,
    col,
    row,
    out,
    diff,
    summ,
):
    size = out.shape[-1]
    step = pl.program_id(0)
    half = size // 2

    @pl.when(step == 0)
    def _():
        fill_masks(col, row, diff, summ)

        def clear(j, carry):
            out[0, j] = jnp.zeros((size, size), jnp.float32)
            out[1, j] = jnp.zeros((size, size), jnp.float32)
            return carry

        lax.fori_loop(0, out.shape[1], clear, 0)

        def operator(n, carry):
            def term(c, inner):
                j, s, amp = target[n, c], site[n, c], alpha[n, c]
                for part in range(2):
                    rows = pl.ds(part * half, half)
                    weight = amp * diff[s, rows]
                    out[0, j, rows] += weight * y_band[n, 1, rows]
                    out[1, j, rows] -= weight * y_band[n, 0, rows]
                return inner

            return lax.fori_loop(0, count[n], term, carry)

        lax.fori_loop(0, y_band.shape[0], operator, 0)

    @pl.when(own_int[step, 0] == 1)
    def _():
        j, s = own_op[step], own_int[step, 1]
        damping, amp, amp_cos, amp_sin = (own_flt[step, i] for i in range(4))
        own = rho_own[:, 0] + section_weight * kprev_own[:, 0]
        real, imag = commutator(left[...], right[...], own)
        top = rho_top[:, 0] + section_weight * kprev_top[:, 0]
        w_re, w_im = amp_cos * diff[s], amp_sin * summ[s]
        out[0, j] += imag - damping * own[0] + (w_re * top[1] + w_im * top[0])
        out[1, j] += -real - damping * own[1] + (w_im * top[1] - w_re * top[0])
        up = amp * diff[s]
        out[0, 0] += up * own[1]
        out[1, 0] -= up * own[0]


def add_terms(n, rows, count, source, site, alpha, beta, fetch, diff, summ, start):
    def term(c, state):
        re, im = state
        m, s = source[n, c], site[n, c]
        w_re = alpha[n, c] * diff[s, rows]
        w_im = beta[n, c] * summ[s, rows]
        y_re, y_im = fetch(m, rows)
        return re + (w_re * y_im + w_im * y_re), im + (w_im * y_im - w_re * y_re)

    return lax.fori_loop(0, count[n], term, start)


def local_kernel(
    count,
    source,
    site,
    alpha,
    beta,
    damping,
    y_band,
    rho_low,
    kprev_low,
    left,
    right,
    col,
    row,
    out,
    pool,
    diff,
    summ,
):
    size = out.shape[-1]
    low_count, band_count = rho_low.shape[1], y_band.shape[0]
    half = size // 2
    fill_masks(col, row, diff, summ)

    def advance(i, carry):
        for part in range(2):
            pool[i, part] = rho_low[part, i] + section_weight * kprev_low[part, i]
        return carry

    lax.fori_loop(0, low_count, advance, 0)

    def keep(i, carry):
        pool[low_count + i] = y_band[i]
        return carry

    lax.fori_loop(0, band_count, keep, 0)

    def operator(n, carry):
        y_pair = y_band[n]
        real, imag = commutator(left[...], right[...], y_pair)
        out[0, n] = imag - damping[n] * y_pair[0]
        out[1, n] = -real - damping[n] * y_pair[1]
        for part in range(2):
            rows = pl.ds(part * half, half)
            re, im = add_terms(
                n,
                rows,
                count,
                source,
                site,
                alpha,
                beta,
                lambda m, r: (pool[m, 0, r], pool[m, 1, r]),
                diff,
                summ,
                (out[0, n, rows], out[1, n, rows]),
            )
            out[0, n, rows] = re
            out[1, n, rows] = im
        return carry

    lax.fori_loop(0, band_count, operator, 0)


def far_kernel(
    count, source, site, alpha, beta, received, base, col, row, out, diff, summ
):
    sites, block, size = diff.shape
    step = pl.program_id(0)

    def one_site(s, carry):
        va = jnp.where(col[...] == s, 1.0, 0.0)
        vb = jnp.where(row[...] == s, 1.0, 0.0)
        va = jnp.broadcast_to(va, (block, size))
        vb = jnp.broadcast_to(vb, (block, size))
        diff[s] = va - vb
        summ[s] = va + vb
        return carry

    lax.fori_loop(0, sites, one_site, 0)
    rows = pl.ds(0, block)

    def operator(n, carry):
        re, im = add_terms(
            n,
            rows,
            count,
            source,
            site,
            alpha,
            beta,
            lambda m, r: (received[m, 0, r], received[m, 1, r]),
            diff,
            summ,
            (base[0, n], base[1, n]),
        )
        out[0, n] = re
        out[1, n] = im
        return carry

    lax.fori_loop(0, out.shape[1], operator, 0)


def compact(flag, arrays):
    width = flag.shape[1]
    place = jnp.cumsum(flag.astype(jnp.int32), axis=1) - 1
    hit = (place[:, :, None] == jnp.arange(width)[None, None, :]) & flag[:, :, None]
    packed = [jnp.sum(jnp.where(hit, a[:, :, None], 0), axis=1).astype(a.dtype) for a in arrays]
    return jnp.sum(flag.astype(jnp.int32), axis=1), packed


def pick(index, table):
    hit = index[..., None] == jnp.arange(table.shape[-1], dtype=index.dtype)
    return jnp.sum(jnp.where(hit, table, 0), axis=-1).astype(table.dtype)


def shards(
    rho_low,
    kprev_low,
    rho_band,
    kprev_band,
    hamiltonian,
    state_site,
    coupling_mag,
    coupling_phase,
    damping_rate,
    low_mode,
    occupation,
    couple_src,
    couple_mode,
    couple_dir,
):
    band_size = lax.axis_size("band")
    own_index = lax.axis_index("band")
    low_count = rho_low.shape[1]
    band_count = rho_band.shape[1]
    size = rho_band.shape[-1]
    modes = coupling_mag.shape[0]
    sites = modes // EXPS
    f32 = jnp.float32
    params = functools.partial(pltpu.CompilerParams, vmem_limit_bytes=VMEM_LIMIT)

    shifted = couple_src - low_count
    owner = jnp.where(couple_src >= low_count, shifted // band_count, own_index)
    remote = owner != own_index
    slot = shifted % band_count
    asks = remote[None] & (owner[None] == jnp.arange(band_size)[:, None, None])
    wanted = jnp.max(jnp.where(asks, slot[None], 0), axis=(1, 2))
    asked = lax.all_to_all(wanted, "band", split_axis=0, concat_axis=0, tiled=True)

    y_band, send = pl.pallas_call(
        send_kernel,
        in_specs=[smem, vmem, vmem],
        out_specs=[vmem, hbm],
        out_shape=[
            jax.ShapeDtypeStruct((band_count, 2, size, size), f32),
            jax.ShapeDtypeStruct((band_size, 2, size, size), f32),
        ],
        scratch_shapes=[pltpu.SemaphoreType.DMA((band_size,))],
        compiler_params=params(),
        name="send",
    )(asked, rho_band, kprev_band)
    received = lax.all_to_all(send, "band", split_axis=0, concat_axis=0, tiled=True)

    level = jnp.sum(
        jnp.where(
            couple_mode[:, :, None] == jnp.arange(modes)[None, None, :],
            occupation[:, None, :],
            0,
        ),
        axis=-1,
    ).astype(f32)
    strength = pick(couple_mode, coupling_mag)
    cos_mode, sin_mode = jnp.cos(coupling_phase), jnp.sin(coupling_phase)
    is_down = couple_dir == 1
    amp_down = jnp.sqrt(level * strength)
    alpha = jnp.where(
        is_down, amp_down * pick(couple_mode, cos_mode), jnp.sqrt((level + 1.0) * strength)
    )
    beta = jnp.where(is_down, amp_down * pick(couple_mode, sin_mode), 0.0)
    site = couple_mode // EXPS
    live = couple_src >= 0
    is_low = live & (couple_src < low_count)
    position = jnp.where(couple_src < low_count, couple_src, low_count + slot)
    marks = jnp.concatenate([jnp.full((1,), -1, jnp.int32), low_mode])
    held = (pick(jnp.clip(couple_src, 0, low_count - 1), marks) == couple_mode).astype(f32)
    alpha_low = jnp.sqrt((held + 1.0) * strength)
    damping = jnp.dot(occupation.astype(f32), damping_rate, precision=highest)
    low_n, (low_j, low_s, low_a) = compact(is_low, [couple_src, site, alpha_low])
    near_n, near = compact(live & ~remote, [position, site, alpha, beta])
    far_n, far = compact(live & remote, [owner, site, alpha, beta])

    h_re, h_im = hamiltonian[0], hamiltonian[1]
    left = jnp.block([[h_re, -h_im], [h_im, h_re]])
    right = jnp.block([[h_re, h_im], [-h_im, h_re]])
    col, row = state_site[:, None], state_site[None, :]

    turns = -(-low_count // band_size)
    own_op = own_index + band_size * jnp.arange(turns, dtype=jnp.int32)
    own_here = own_op < low_count
    own_op = jnp.minimum(own_op, low_count - 1)
    own_mode = pick(jnp.maximum(own_op - 1, 0), low_mode)
    raised = (own_op >= 1).astype(f32)
    own_amp = jnp.sqrt(pick(own_mode, coupling_mag)) * raised
    own_int = jnp.stack([own_here.astype(jnp.int32), own_mode // EXPS], axis=1)
    own_flt = jnp.stack(
        [
            pick(own_mode, damping_rate) * raised,
            own_amp,
            own_amp * pick(own_mode, cos_mode),
            own_amp * pick(own_mode, sin_mode),
        ],
        axis=1,
    )
    own_block = pl.BlockSpec((2, 1, size, size), lambda g, ops: (0, ops[g], 0, 0))
    top_block = pl.BlockSpec((2, 1, size, size), lambda g, ops: (0, 0, 0, 0))
    partial = pl.pallas_call(
        low_kernel,
        grid_spec=pltpu.PrefetchScalarGridSpec(
            num_scalar_prefetch=1,
            grid=(turns,),
            in_specs=[smem] * 6
            + [vmem, own_block, own_block, top_block, top_block]
            + [vmem] * 4,
            out_specs=vmem,
            scratch_shapes=[pltpu.VMEM((sites, size, size), f32)] * 2,
        ),
        out_shape=jax.ShapeDtypeStruct((2, low_count, size, size), f32),
        compiler_params=params(),
        name="low",
    )(
        own_op,
        own_int,
        own_flt,
        low_n,
        low_j,
        low_s,
        low_a,
        y_band,
        rho_low,
        kprev_low,
        rho_low,
        kprev_low,
        left,
        right,
        col,
        row,
    )
    k_low = lax.psum(partial, "band")

    base = pl.pallas_call(
        local_kernel,
        in_specs=[smem] * 6 + [vmem] * 7,
        out_specs=vmem,
        out_shape=jax.ShapeDtypeStruct((2, band_count, size, size), f32),
        scratch_shapes=[pltpu.VMEM((low_count + band_count, 2, size, size), f32)]
        + [pltpu.VMEM((sites, size, size), f32)] * 2,
        compiler_params=params(),
        name="local",
    )(near_n, *near, damping, y_band, rho_low, kprev_low, left, right, col, row)

    block = size // 2
    k_band = pl.pallas_call(
        far_kernel,
        grid=(size // block,),
        in_specs=[smem] * 5
        + [
            pl.BlockSpec((band_size, 2, block, size), lambda g: (0, 0, g, 0)),
            pl.BlockSpec((2, band_count, block, size), lambda g: (0, 0, g, 0)),
            pl.BlockSpec((block, 1), lambda g: (g, 0)),
            pl.BlockSpec((1, size), lambda g: (0, 0)),
        ],
        out_specs=pl.BlockSpec((2, band_count, block, size), lambda g: (0, 0, g, 0)),
        out_shape=jax.ShapeDtypeStruct((2, band_count, size, size), f32),
        scratch_shapes=[pltpu.VMEM((sites, block, size), f32)] * 2,
        compiler_params=params(),
        name="far",
    )(far_n, *far, received, base, col, row)
    return (k_low, k_band)


def solution(mesh):
    placed = (
        P(),
        P(),
        P(None, "band", None, None),
        P(None, "band", None, None),
        P(),
        P(),
        P(),
        P(),
        P(),
        P(),
        P("band", None),
        P("band", None),
        P("band", None),
        P("band", None),
    )
    return jax.shard_map(
        shards,
        mesh=mesh,
        in_specs=placed,
        out_specs=(P(), P(None, "band", None, None)),
        check_vma=False,
    )
```

```python
import functools

import jax
import jax.numpy as jnp
from jax import lax
from jax.experimental import pallas as pl
from jax.experimental.pallas import tpu as pltpu
from jax.sharding import PartitionSpec as P

EXPS = 3
section_weight = 0.2
highest = lax.Precision.HIGHEST
VMEM_LIMIT = 60 * 1024 * 1024

vmem = pl.BlockSpec(memory_space=pltpu.VMEM)
smem = pl.BlockSpec(memory_space=pltpu.SMEM)
hbm = pl.BlockSpec(memory_space=pl.ANY)


def fill_masks(col_ref, row_ref, diff_ref, sum_ref):
    sites, size = diff_ref.shape[0], diff_ref.shape[1]

    def one_site(s, carry):
        va = jnp.where(col_ref[...] == s, 1.0, 0.0)
        vb = jnp.where(row_ref[...] == s, 1.0, 0.0)
        va = jnp.broadcast_to(va, (size, size))
        vb = jnp.broadcast_to(vb, (size, size))
        diff_ref[s] = va - vb
        if sum_ref is not None:
            sum_ref[s] = va + vb
        return carry

    lax.fori_loop(0, sites, one_site, 0)


def commutator(left, right, y_pair):
    size = y_pair.shape[-1]
    lhs = jnp.dot(
        left,
        y_pair.reshape(2 * size, size),
        precision=highest,
        preferred_element_type=jnp.float32,
    )
    rhs = jnp.dot(
        jnp.concatenate([y_pair[0], y_pair[1]], axis=1),
        right,
        precision=highest,
        preferred_element_type=jnp.float32,
    )
    return lhs[:size] - rhs[:, :size], lhs[size:] - rhs[:, size:]


LOW_J, LOW_S, NEAR_M, NEAR_S, FAR_M, FAR_S, COUNTS, OWN_I = range(8)
LOW_A, NEAR_A, NEAR_B, FAR_A, FAR_B, DAMP, OWN_F = range(7)


def prep_kernel(
    low_count, own, src, mode, direction, occ, mag, cos, sin, rate, low_mode, ints, flts
):
    rows, width = src.shape
    modes = occ.shape[1]
    others = low_mode.shape[1]
    band_size = own[1]
    own_index = own[0]
    f32, i32 = jnp.float32, jnp.int32
    lane_mode = lax.broadcasted_iota(i32, (rows, modes), 1)
    lane_low = lax.broadcasted_iota(i32, (rows, others), 1)
    lane_col = lax.broadcasted_iota(i32, (rows, width), 1)
    occ_f = occ[...].astype(f32)
    mag_b = jnp.broadcast_to(mag[...], (rows, modes))
    cos_b = jnp.broadcast_to(cos[...], (rows, modes))
    sin_b = jnp.broadcast_to(sin[...], (rows, modes))
    rate_b = jnp.broadcast_to(rate[...], (rows, modes))
    mark_b = jnp.broadcast_to(low_mode[...].astype(f32) + 1.0, (rows, others))

    def total(x):
        return jnp.sum(x, axis=1, keepdims=True)

    zero_i = jnp.zeros((rows, width), i32)
    zero_f = jnp.zeros((rows, width), f32)
    int_out = [zero_i] * 6
    flt_out = [zero_f] * 5
    fill = [jnp.zeros((rows, 1), i32)] * 3
    for c in range(width):
        src_c, mode_c = src[:, c : c + 1], mode[:, c : c + 1]
        down = direction[:, c : c + 1] == 1
        hit = lane_mode == mode_c
        level = total(jnp.where(hit, occ_f, 0.0))
        strength = total(jnp.where(hit, mag_b, 0.0))
        amp_down = jnp.sqrt(level * strength)
        amp_up = jnp.sqrt((level + 1.0) * strength)
        alpha = jnp.where(down, amp_down * total(jnp.where(hit, cos_b, 0.0)), amp_up)
        beta = jnp.where(down, amp_down * total(jnp.where(hit, sin_b, 0.0)), 0.0)
        mark = total(jnp.where(lane_low == src_c - 1, mark_b, 0.0))
        held = jnp.where(mark == mode_c.astype(f32) + 1.0, 2.0, 1.0)
        alpha_low = jnp.sqrt(held * strength)
        site = mode_c // EXPS
        live = src_c >= 0
        is_low = live & (src_c < low_count)
        shifted = jnp.maximum(src_c - low_count, 0)
        owner = shifted // rows
        local = is_low | (live & (owner == own_index))
        near_m = jnp.where(is_low, src_c, low_count + shifted % rows)
        lists = (
            (is_low, (src_c, site), (alpha_low,)),
            (local, (near_m, site), (alpha, beta)),
            (live & ~local, (owner, site), (alpha, beta)),
        )
        at_f = 0
        for which, (flag, int_cols, flt_cols) in enumerate(lists):
            put = (lane_col == fill[which]) & flag
            for i, value in enumerate(int_cols):
                int_out[2 * which + i] = int_out[2 * which + i] + jnp.where(put, value, 0)
            for value in flt_cols:
                flt_out[at_f] = flt_out[at_f] + jnp.where(put, value, 0.0)
                at_f += 1
            fill[which] = fill[which] + jnp.where(flag, 1, 0)
    for i in range(6):
        ints[i] = int_out[i]
    for i in range(5):
        flts[i] = flt_out[i]
    ints[COUNTS] = jnp.where(
        lane_col == 0, fill[0], jnp.where(lane_col == 1, fill[1], fill[2])
    )
    flts[DAMP] = jnp.broadcast_to(total(occ_f * rate_b), (rows, width))
    turn = lax.broadcasted_iota(i32, (rows, 1), 0)
    op = own_index + band_size * turn
    here = jnp.where(op < low_count, 1, 0)
    op = jnp.minimum(op, low_count - 1)
    op_mode = total(jnp.where(lane_low == jnp.maximum(op - 1, 0), mark_b, 0.0)) - 1.0
    op_mode = op_mode.astype(i32)
    hit = lane_mode == op_mode
    raised = jnp.where(op >= 1, 1.0, 0.0)
    amp = jnp.sqrt(total(jnp.where(hit, mag_b, 0.0))) * raised
    amp_cos = amp * total(jnp.where(hit, cos_b, 0.0))
    amp_sin = amp * total(jnp.where(hit, sin_b, 0.0))
    damp = total(jnp.where(hit, rate_b, 0.0)) * raised
    ints[OWN_I] = jnp.where(lane_col == 0, here, jnp.where(lane_col == 1, op_mode // EXPS, op))
    flts[OWN_F] = jnp.where(
        lane_col == 0,
        damp,
        jnp.where(lane_col == 1, amp, jnp.where(lane_col == 2, amp_cos, amp_sin)),
    )


def send_kernel(asked, rho, kprev, y_out, send, sems):
    count = rho.shape[1]
    peers = send.shape[0]

    def advance(i, carry):
        for part in range(2):
            y_out[i, part] = rho[part, i] + section_weight * kprev[part, i]
        return carry

    lax.fori_loop(0, count, advance, 0)

    def start(i, carry):
        pltpu.make_async_copy(y_out.at[asked[i, 0, 0]], send.at[i], sems.at[i]).start()
        return carry

    def finish(i, carry):
        pltpu.make_async_copy(y_out.at[0], send.at[i], sems.at[i]).wait()
        return carry

    lax.fori_loop(0, peers, start, 0)
    lax.fori_loop(0, peers, finish, 0)


def low_kernel(
    ints,
    flts,
    y_band,
    rho_own,
    kprev_own,
    rho_top,
    kprev_top,
    left,
    right,
    col,
    row,
    out,
    diff,
    summ,
):
    size = out.shape[-1]
    step = pl.program_id(0)
    half = size // 2

    @pl.when(step == 0)
    def _():
        fill_masks(col, row, diff, summ)

        def clear(j, carry):
            out[0, j] = jnp.zeros((size, size), jnp.float32)
            out[1, j] = jnp.zeros((size, size), jnp.float32)
            return carry

        lax.fori_loop(0, out.shape[1], clear, 0)

        def operator(n, carry):
            def term(c, inner):
                j, s, amp = ints[LOW_J, n, c], ints[LOW_S, n, c], flts[LOW_A, n, c]
                for part in range(2):
                    rows = pl.ds(part * half, half)
                    weight = amp * diff[s, rows]
                    out[0, j, rows] += weight * y_band[n, 1, rows]
                    out[1, j, rows] -= weight * y_band[n, 0, rows]
                return inner

            return lax.fori_loop(0, ints[COUNTS, n, 0], term, carry)

        lax.fori_loop(0, y_band.shape[0], operator, 0)

    @pl.when(ints[OWN_I, step, 0] == 1)
    def _():
        s, j = ints[OWN_I, step, 1], ints[OWN_I, step, 2]
        damping, amp, amp_cos, amp_sin = (flts[OWN_F, step, i] for i in range(4))
        own = rho_own[:, 0] + section_weight * kprev_own[:, 0]
        real, imag = commutator(left[...], right[...], own)
        top = rho_top[:, 0] + section_weight * kprev_top[:, 0]
        w_re, w_im = amp_cos * diff[s], amp_sin * summ[s]
        out[0, j] += imag - damping * own[0] + (w_re * top[1] + w_im * top[0])
        out[1, j] += -real - damping * own[1] + (w_im * top[1] - w_re * top[0])
        up = amp * diff[s]
        out[0, 0] += up * own[1]
        out[1, 0] -= up * own[0]


def add_terms(n, rows, which, ints, flts, fetch, diff, summ, start):
    count_at, source_at, alpha_at = which

    def term(c, state):
        re, im = state
        m, s = ints[source_at, n, c], ints[source_at + 1, n, c]
        w_re = flts[alpha_at, n, c] * diff[s, rows]
        w_im = flts[alpha_at + 1, n, c] * summ[s, rows]
        y_re, y_im = fetch(m, rows)
        return re + (w_re * y_im + w_im * y_re), im + (w_im * y_im - w_re * y_re)

    return lax.fori_loop(0, ints[COUNTS, n, count_at], term, start)


def local_kernel(
    ints,
    flts,
    y_band,
    rho_low,
    kprev_low,
    left,
    right,
    col,
    row,
    out,
    pool,
    diff,
    summ,
):
    size = out.shape[-1]
    low_count, band_count = rho_low.shape[1], y_band.shape[0]
    half = size // 2
    fill_masks(col, row, diff, summ)

    def advance(i, carry):
        for part in range(2):
            pool[i, part] = rho_low[part, i] + section_weight * kprev_low[part, i]
        return carry

    lax.fori_loop(0, low_count, advance, 0)

    def keep(i, carry):
        pool[low_count + i] = y_band[i]
        return carry

    lax.fori_loop(0, band_count, keep, 0)

    def operator(n, carry):
        y_pair = y_band[n]
        damping = flts[DAMP, n, 0]
        real, imag = commutator(left[...], right[...], y_pair)
        out[0, n] = imag - damping * y_pair[0]
        out[1, n] = -real - damping * y_pair[1]
        for part in range(2):
            rows = pl.ds(part * half, half)
            re, im = add_terms(
                n,
                rows,
                (1, NEAR_M, NEAR_A),
                ints,
                flts,
                lambda m, r: (pool[m, 0, r], pool[m, 1, r]),
                diff,
                summ,
                (out[0, n, rows], out[1, n, rows]),
            )
            out[0, n, rows] = re
            out[1, n, rows] = im
        return carry

    lax.fori_loop(0, band_count, operator, 0)


def far_kernel(ints, flts, received, base, col, row, out, diff, summ):
    sites, block, size = diff.shape

    def one_site(s, carry):
        va = jnp.where(col[...] == s, 1.0, 0.0)
        vb = jnp.where(row[...] == s, 1.0, 0.0)
        va = jnp.broadcast_to(va, (block, size))
        vb = jnp.broadcast_to(vb, (block, size))
        diff[s] = va - vb
        summ[s] = va + vb
        return carry

    lax.fori_loop(0, sites, one_site, 0)
    rows = pl.ds(0, block)

    def operator(n, carry):
        re, im = add_terms(
            n,
            rows,
            (2, FAR_M, FAR_A),
            ints,
            flts,
            lambda m, r: (received[m, 0, r], received[m, 1, r]),
            diff,
            summ,
            (base[0, n], base[1, n]),
        )
        out[0, n] = re
        out[1, n] = im
        return carry

    lax.fori_loop(0, out.shape[1], operator, 0)


def sum_over_band(rows, band_size, own_index):
    bits = band_size.bit_length() - 1
    if 1 << bits != band_size or rows.shape[0] % (2 * band_size * 8):
        return lax.psum(rows, "band")
    plain = list(range(bits))
    swapped = plain[:1] + plain[1:3][::-1] + plain[3:]
    orders = (plain, swapped)
    stream = rows.shape[0] // 2
    starts = [jnp.int32(0), jnp.int32(stream)]
    length = stream
    flag = [(own_index >> b) & 1 for b in range(bits)]

    def swap(x, bit):
        pairs = [(i, i ^ (1 << bit)) for i in range(band_size)]
        return lax.ppermute(x, "band", pairs)

    for level in range(bits):
        length //= 2
        got, keep = [], []
        for order, start in zip(orders, starts):
            mine = flag[order[level]]
            give = lax.dynamic_slice_in_dim(rows, start + (1 - mine) * length, length)
            got.append(swap(give, order[level]))
            keep.append(start + mine * length)
        for other, start in zip(got, keep):
            held = lax.dynamic_slice_in_dim(rows, start, length)
            rows = lax.dynamic_update_slice_in_dim(rows, held + other, start, 0)
        starts = keep
    for level in reversed(range(bits)):
        got = []
        for order, start in zip(orders, starts):
            got.append(swap(lax.dynamic_slice_in_dim(rows, start, length), order[level]))
        moved = []
        for order, start, other in zip(orders, starts, got):
            mine = flag[order[level]]
            base = start - mine * length
            rows = lax.dynamic_update_slice_in_dim(rows, other, base + (1 - mine) * length, 0)
            moved.append(base)
        starts = moved
        length *= 2
    return rows


def shards(
    rho_low,
    kprev_low,
    rho_band,
    kprev_band,
    hamiltonian,
    state_site,
    coupling_mag,
    coupling_phase,
    damping_rate,
    low_mode,
    occupation,
    couple_src,
    couple_mode,
    couple_dir,
):
    band_size = lax.axis_size("band")
    own_index = lax.axis_index("band")
    low_count = rho_low.shape[1]
    band_count = rho_band.shape[1]
    size = rho_band.shape[-1]
    sites = coupling_mag.shape[0] // EXPS
    f32 = jnp.float32
    params = functools.partial(pltpu.CompilerParams, vmem_limit_bytes=VMEM_LIMIT)

    shifted = couple_src - low_count
    owner = jnp.where(couple_src >= low_count, shifted // band_count, own_index)
    slot = jnp.where(owner != own_index, shifted % band_count, 0)
    asks = owner[None] == jnp.arange(band_size)[:, None, None]
    wanted = jnp.max(jnp.where(asks, slot[None], 0), axis=(1, 2))
    wanted = jnp.broadcast_to(wanted[:, None, None], (band_size, 1, 128))
    asked = lax.all_to_all(wanted, "band", split_axis=0, concat_axis=0, tiled=True)

    y_band, send = pl.pallas_call(
        send_kernel,
        in_specs=[smem, vmem, vmem],
        out_specs=[vmem, hbm],
        out_shape=[
            jax.ShapeDtypeStruct((band_count, 2, size, size), f32),
            jax.ShapeDtypeStruct((band_size, 2, size, size), f32),
        ],
        scratch_shapes=[pltpu.SemaphoreType.DMA((band_size,))],
        compiler_params=params(),
        name="send",
    )(asked, rho_band, kprev_band)
    received = lax.all_to_all(send, "band", split_axis=0, concat_axis=0, tiled=True)

    whole_row = (1, -1)
    own = jnp.stack([own_index, jnp.int32(band_size)]).astype(jnp.int32)
    ints, flts = pl.pallas_call(
        functools.partial(prep_kernel, low_count),
        in_specs=[smem] + [vmem] * 9,
        out_specs=[vmem, vmem],
        out_shape=[
            jax.ShapeDtypeStruct((8,) + couple_src.shape, jnp.int32),
            jax.ShapeDtypeStruct((7,) + couple_src.shape, f32),
        ],
        name="prep",
    )(
        own,
        couple_src,
        couple_mode,
        couple_dir,
        occupation,
        coupling_mag.reshape(whole_row),
        jnp.cos(coupling_phase).reshape(whole_row),
        jnp.sin(coupling_phase).reshape(whole_row),
        damping_rate.reshape(whole_row),
        low_mode.reshape(whole_row),
    )

    h_re, h_im = hamiltonian[0], hamiltonian[1]
    left = jnp.block([[h_re, -h_im], [h_im, h_re]])
    right = jnp.block([[h_re, h_im], [-h_im, h_re]])
    col, row = state_site[:, None], state_site[None, :]

    turns = -(-low_count // band_size)
    own_op = jnp.minimum(
        own_index + band_size * jnp.arange(turns, dtype=jnp.int32), low_count - 1
    )
    own_block = pl.BlockSpec((2, 1, size, size), lambda g, ops: (0, ops[g], 0, 0))
    top_block = pl.BlockSpec((2, 1, size, size), lambda g, ops: (0, 0, 0, 0))
    partial = pl.pallas_call(
        lambda ops, *refs: low_kernel(*refs),
        grid_spec=pltpu.PrefetchScalarGridSpec(
            num_scalar_prefetch=1,
            grid=(turns,),
            in_specs=[smem] * 2
            + [vmem, own_block, own_block, top_block, top_block]
            + [vmem] * 4,
            out_specs=vmem,
            scratch_shapes=[pltpu.VMEM((sites, size, size), f32)] * 2,
        ),
        out_shape=jax.ShapeDtypeStruct((2, low_count, size, size), f32),
        compiler_params=params(),
        name="low",
    )(
        own_op,
        ints,
        flts,
        y_band,
        rho_low,
        kprev_low,
        rho_low,
        kprev_low,
        left,
        right,
        col,
        row,
    )
    k_low = sum_over_band(partial.reshape(-1, size), band_size, own_index)
    k_low = k_low.reshape(partial.shape)

    base = pl.pallas_call(
        local_kernel,
        in_specs=[smem] * 2 + [vmem] * 7,
        out_specs=vmem,
        out_shape=jax.ShapeDtypeStruct((2, band_count, size, size), f32),
        scratch_shapes=[pltpu.VMEM((low_count + band_count, 2, size, size), f32)]
        + [pltpu.VMEM((sites, size, size), f32)] * 2,
        compiler_params=params(),
        name="local",
    )(ints, flts, y_band, rho_low, kprev_low, left, right, col, row)

    block = size // 2
    k_band = pl.pallas_call(
        far_kernel,
        grid=(size // block,),
        in_specs=[smem] * 2
        + [
            pl.BlockSpec((band_size, 2, block, size), lambda g: (0, 0, g, 0)),
            pl.BlockSpec((2, band_count, block, size), lambda g: (0, 0, g, 0)),
            pl.BlockSpec((block, 1), lambda g: (g, 0)),
            pl.BlockSpec((1, size), lambda g: (0, 0)),
        ],
        out_specs=pl.BlockSpec((2, band_count, block, size), lambda g: (0, 0, g, 0)),
        out_shape=jax.ShapeDtypeStruct((2, band_count, size, size), f32),
        scratch_shapes=[pltpu.VMEM((sites, block, size), f32)] * 2,
        compiler_params=params(),
        name="far",
    )(ints, flts, received, base, col, row)
    return (k_low, k_band)


def solution(mesh):
    placed = (
        P(),
        P(),
        P(None, "band", None, None),
        P(None, "band", None, None),
        P(),
        P(),
        P(),
        P(),
        P(),
        P(),
        P("band", None),
        P("band", None),
        P("band", None),
        P("band", None),
    )
    return jax.shard_map(
        shards,
        mesh=mesh,
        in_specs=placed,
        out_specs=(P(), P(None, "band", None, None)),
        check_vma=False,
    )
```

```python
import functools

import jax
import jax.numpy as jnp
from jax import lax
from jax.experimental import pallas as pl
from jax.experimental.pallas import tpu as pltpu
from jax.sharding import PartitionSpec as P

EXPS = 3
OUTER = 4
BLOCKS = 4
section_weight = 0.2
highest = lax.Precision.HIGHEST
VMEM_LIMIT = 60 * 1024 * 1024

vmem = pl.BlockSpec(memory_space=pltpu.VMEM)
smem = pl.BlockSpec(memory_space=pltpu.SMEM)
hbm = pl.BlockSpec(memory_space=pl.ANY)


def fill_masks(col_ref, row_ref, diff_ref, sum_ref):
    sites, size = diff_ref.shape[0], diff_ref.shape[1]

    def one_site(s, carry):
        va = jnp.where(col_ref[...] == s, 1.0, 0.0)
        vb = jnp.where(row_ref[...] == s, 1.0, 0.0)
        va = jnp.broadcast_to(va, (size, size))
        vb = jnp.broadcast_to(vb, (size, size))
        diff_ref[s] = va - vb
        if sum_ref is not None:
            sum_ref[s] = va + vb
        return carry

    lax.fori_loop(0, sites, one_site, 0)


def commutator(left, right, y_pair):
    size = y_pair.shape[-1]
    lhs = jnp.dot(
        left,
        y_pair.reshape(2 * size, size),
        precision=highest,
        preferred_element_type=jnp.float32,
    )
    rhs = jnp.dot(
        jnp.concatenate([y_pair[0], y_pair[1]], axis=1),
        right,
        precision=highest,
        preferred_element_type=jnp.float32,
    )
    return lhs[:size] - rhs[:, :size], lhs[size:] - rhs[:, size:]


LOW_J, LOW_S, NEAR_M, NEAR_S, FAR_M, FAR_S, COUNTS, OWN_I = range(8)
LOW_A, NEAR_A, NEAR_B, FAR_A, FAR_B, DAMP, OWN_F = range(7)


def prep_kernel(
    low_count, own, src, mode, direction, occ, mag, cos, sin, rate, low_mode, ints, flts
):
    rows, width = src.shape
    modes = occ.shape[1]
    others = low_mode.shape[1]
    own_index, band_size, inner = own[0], own[1], own[2]
    f32, i32 = jnp.float32, jnp.int32
    lane_mode = lax.broadcasted_iota(i32, (rows, modes), 1)
    lane_low = lax.broadcasted_iota(i32, (rows, others), 1)
    lane_col = lax.broadcasted_iota(i32, (rows, width), 1)
    occ_f = occ[...].astype(f32)
    mag_b = jnp.broadcast_to(mag[...], (rows, modes))
    cos_b = jnp.broadcast_to(cos[...], (rows, modes))
    sin_b = jnp.broadcast_to(sin[...], (rows, modes))
    rate_b = jnp.broadcast_to(rate[...], (rows, modes))
    mark_b = jnp.broadcast_to(low_mode[...].astype(f32) + 1.0, (rows, others))

    def total(x):
        return jnp.sum(x, axis=1, keepdims=True)

    zero_i = jnp.zeros((rows, width), i32)
    zero_f = jnp.zeros((rows, width), f32)
    int_out = [zero_i] * 6
    flt_out = [zero_f] * 5
    fill = [jnp.zeros((rows, 1), i32)] * 3
    for c in range(width):
        src_c, mode_c = src[:, c : c + 1], mode[:, c : c + 1]
        down = direction[:, c : c + 1] == 1
        hit = lane_mode == mode_c
        level = total(jnp.where(hit, occ_f, 0.0))
        strength = total(jnp.where(hit, mag_b, 0.0))
        amp_down = jnp.sqrt(level * strength)
        amp_up = jnp.sqrt((level + 1.0) * strength)
        alpha = jnp.where(down, amp_down * total(jnp.where(hit, cos_b, 0.0)), amp_up)
        beta = jnp.where(down, amp_down * total(jnp.where(hit, sin_b, 0.0)), 0.0)
        mark = total(jnp.where(lane_low == src_c - 1, mark_b, 0.0))
        held = jnp.where(mark == mode_c.astype(f32) + 1.0, 2.0, 1.0)
        alpha_low = jnp.sqrt(held * strength)
        site = mode_c // EXPS
        live = src_c >= 0
        is_low = live & (src_c < low_count)
        shifted = jnp.maximum(src_c - low_count, 0)
        owner = shifted // rows
        local = is_low | (live & (owner == own_index))
        outer = band_size // inner
        far_m = (owner % inner) * outer + ((owner // inner) ^ (own_index // inner))
        near_m = jnp.where(is_low, src_c, low_count + shifted % rows)
        lists = (
            (is_low, (src_c, site), (alpha_low,)),
            (local, (near_m, site), (alpha, beta)),
            (live & ~local, (far_m, site), (alpha, beta)),
        )
        at_f = 0
        for which, (flag, int_cols, flt_cols) in enumerate(lists):
            put = (lane_col == fill[which]) & flag
            for i, value in enumerate(int_cols):
                int_out[2 * which + i] = int_out[2 * which + i] + jnp.where(put, value, 0)
            for value in flt_cols:
                flt_out[at_f] = flt_out[at_f] + jnp.where(put, value, 0.0)
                at_f += 1
            fill[which] = fill[which] + jnp.where(flag, 1, 0)
    for i in range(6):
        ints[i] = int_out[i]
    for i in range(5):
        flts[i] = flt_out[i]
    ints[COUNTS] = jnp.where(
        lane_col == 0, fill[0], jnp.where(lane_col == 1, fill[1], fill[2])
    )
    flts[DAMP] = jnp.broadcast_to(total(occ_f * rate_b), (rows, width))
    turn = lax.broadcasted_iota(i32, (rows, 1), 0)
    op = own_index + band_size * turn
    here = jnp.where(op < low_count, 1, 0)
    op = jnp.minimum(op, low_count - 1)
    op_mode = total(jnp.where(lane_low == jnp.maximum(op - 1, 0), mark_b, 0.0)) - 1.0
    op_mode = op_mode.astype(i32)
    hit = lane_mode == op_mode
    raised = jnp.where(op >= 1, 1.0, 0.0)
    amp = jnp.sqrt(total(jnp.where(hit, mag_b, 0.0))) * raised
    amp_cos = amp * total(jnp.where(hit, cos_b, 0.0))
    amp_sin = amp * total(jnp.where(hit, sin_b, 0.0))
    damp = total(jnp.where(hit, rate_b, 0.0)) * raised
    ints[OWN_I] = jnp.where(lane_col == 0, here, jnp.where(lane_col == 1, op_mode // EXPS, op))
    flts[OWN_F] = jnp.where(
        lane_col == 0,
        damp,
        jnp.where(lane_col == 1, amp, jnp.where(lane_col == 2, amp_cos, amp_sin)),
    )


def send_kernel(own, asked, rho, kprev, y_out, *rest):
    *outs, sems = rest
    count = rho.shape[1]
    inner = outs[0].shape[0]
    outer = asked.shape[0] // inner
    blocks = len(outs) // outer
    height = outs[0].shape[2]

    def advance(i, carry):
        for part in range(2):
            y_out[i, part] = rho[part, i] + section_weight * kprev[part, i]
        return carry

    lax.fori_loop(0, count, advance, 0)
    place = own[0] // inner

    def copy(block, step, p, entry):
        rows = pl.ds(block * height, height)
        out = outs[block * outer + step]
        return pltpu.make_async_copy(
            y_out.at[entry, :, rows], out.at[p], sems.at[block, step * inner + p]
        )

    for block in range(blocks):
        for step in range(outer):

            def start(p, carry):
                copy(block, step, p, asked[(place ^ step) * inner + p, 0, 0]).start()
                return carry

            lax.fori_loop(0, inner, start, 0)
    for block in range(blocks):
        for step in range(outer):

            def finish(p, carry):
                copy(block, step, p, 0).wait()
                return carry

            lax.fori_loop(0, inner, finish, 0)


def low_kernel(
    ints,
    flts,
    y_band,
    rho_own,
    kprev_own,
    rho_top,
    kprev_top,
    left,
    right,
    col,
    row,
    out,
    diff,
    summ,
):
    size = out.shape[-1]
    step = pl.program_id(0)
    half = size // 2

    @pl.when(step == 0)
    def _():
        fill_masks(col, row, diff, summ)

        def clear(j, carry):
            out[0, j] = jnp.zeros((size, size), jnp.float32)
            out[1, j] = jnp.zeros((size, size), jnp.float32)
            return carry

        lax.fori_loop(0, out.shape[1], clear, 0)

        def operator(n, carry):
            def term(c, inner):
                j, s, amp = ints[LOW_J, n, c], ints[LOW_S, n, c], flts[LOW_A, n, c]
                for part in range(2):
                    rows = pl.ds(part * half, half)
                    weight = amp * diff[s, rows]
                    out[0, j, rows] += weight * y_band[n, 1, rows]
                    out[1, j, rows] -= weight * y_band[n, 0, rows]
                return inner

            return lax.fori_loop(0, ints[COUNTS, n, 0], term, carry)

        lax.fori_loop(0, y_band.shape[0], operator, 0)

    @pl.when(ints[OWN_I, step, 0] == 1)
    def _():
        s, j = ints[OWN_I, step, 1], ints[OWN_I, step, 2]
        damping, amp, amp_cos, amp_sin = (flts[OWN_F, step, i] for i in range(4))
        own = rho_own[:, 0] + section_weight * kprev_own[:, 0]
        real, imag = commutator(left[...], right[...], own)
        top = rho_top[:, 0] + section_weight * kprev_top[:, 0]
        w_re, w_im = amp_cos * diff[s], amp_sin * summ[s]
        out[0, j] += imag - damping * own[0] + (w_re * top[1] + w_im * top[0])
        out[1, j] += -real - damping * own[1] + (w_im * top[1] - w_re * top[0])
        up = amp * diff[s]
        out[0, 0] += up * own[1]
        out[1, 0] -= up * own[0]


def add_terms(n, rows, which, ints, flts, fetch, diff, summ, start):
    count_at, source_at, alpha_at = which

    def term(c, state):
        re, im = state
        m, s = ints[source_at, n, c], ints[source_at + 1, n, c]
        w_re = flts[alpha_at, n, c] * diff[s, rows]
        w_im = flts[alpha_at + 1, n, c] * summ[s, rows]
        y_re, y_im = fetch(m, rows)
        return re + (w_re * y_im + w_im * y_re), im + (w_im * y_im - w_re * y_re)

    return lax.fori_loop(0, ints[COUNTS, n, count_at], term, start)


def local_kernel(
    ints,
    flts,
    y_band,
    rho_low,
    kprev_low,
    left,
    right,
    col,
    row,
    out,
    pool,
    diff,
    summ,
):
    size = out.shape[-1]
    low_count, band_count = rho_low.shape[1], y_band.shape[0]
    half = size // 2
    fill_masks(col, row, diff, summ)

    def advance(i, carry):
        for part in range(2):
            pool[i, part] = rho_low[part, i] + section_weight * kprev_low[part, i]
        return carry

    lax.fori_loop(0, low_count, advance, 0)

    def keep(i, carry):
        pool[low_count + i] = y_band[i]
        return carry

    lax.fori_loop(0, band_count, keep, 0)

    def operator(n, carry):
        y_pair = y_band[n]
        damping = flts[DAMP, n, 0]
        real, imag = commutator(left[...], right[...], y_pair)
        out[0, n] = imag - damping * y_pair[0]
        out[1, n] = -real - damping * y_pair[1]
        for part in range(2):
            rows = pl.ds(part * half, half)
            re, im = add_terms(
                n,
                rows,
                (1, NEAR_M, NEAR_A),
                ints,
                flts,
                lambda m, r: (pool[m, 0, r], pool[m, 1, r]),
                diff,
                summ,
                (out[0, n, rows], out[1, n, rows]),
            )
            out[0, n, rows] = re
            out[1, n, rows] = im
        return carry

    lax.fori_loop(0, band_count, operator, 0)


def far_kernel(ints, flts, received, base, col, row, out, diff, summ):
    sites, block, size = diff.shape
    outer = received.shape[1]

    def one_site(s, carry):
        va = jnp.where(col[...] == s, 1.0, 0.0)
        vb = jnp.where(row[...] == s, 1.0, 0.0)
        va = jnp.broadcast_to(va, (block, size))
        vb = jnp.broadcast_to(vb, (block, size))
        diff[s] = va - vb
        summ[s] = va + vb
        return carry

    lax.fori_loop(0, sites, one_site, 0)
    rows = pl.ds(0, block)

    def operator(n, carry):
        re, im = add_terms(
            n,
            rows,
            (2, FAR_M, FAR_A),
            ints,
            flts,
            lambda m, r: (received[m // outer, m % outer, 0], received[m // outer, m % outer, 1]),
            diff,
            summ,
            (base[0, n], base[1, n]),
        )
        out[0, n] = re
        out[1, n] = im
        return carry

    lax.fori_loop(0, out.shape[1], operator, 0)


def part_of(x, index, parts, axis):
    step = x.shape[axis] // parts
    return lax.dynamic_slice_in_dim(x, index * step, step, axis)


def join(pieces, indices, axis):
    shape = list(pieces[0].shape)
    step = shape[axis]
    shape[axis] *= len(pieces)
    out = jnp.zeros(shape, pieces[0].dtype)
    for piece, index in zip(pieces, indices):
        out = lax.dynamic_update_slice_in_dim(out, piece, index * step, axis)
    return out


def sum_over_band(x, band_size, outer, own_index):
    inner = band_size // outer
    bits = inner.bit_length() - 1
    fits = 1 << bits == inner and bits >= 3 and x.shape[1] % (8 * band_size) == 0
    if not fits:
        return lax.psum(x, "band")
    place = own_index // inner
    flag = [(own_index >> b) & 1 for b in range(bits)]
    plain = list(range(1, bits))
    orders = (plain, plain[:2][::-1] + plain[2:])

    def swap(value, distance):
        pairs = [(i, i ^ distance) for i in range(band_size)]
        return lax.ppermute(value, "band", pairs)

    got = swap(part_of(x, 1 - flag[0], 2, 1), 1)
    x = part_of(x, flag[0], 2, 1) + got
    streams = [x[0], x[1]]
    for level in range(bits - 1):
        use = [order[level] for order in orders]
        got = [swap(part_of(v, 1 - flag[b], 2, 0), 1 << b) for v, b in zip(streams, use)]
        streams = [part_of(v, flag[b], 2, 0) + g for v, b, g in zip(streams, use, got)]
    x = jnp.stack(streams)
    got = [swap(part_of(x, place ^ d, outer, 1), d * inner) for d in range(1, outer)]
    x = part_of(x, place, outer, 1)
    for other in got:
        x = x + other
    got = [swap(x, d * inner) for d in range(1, outer)]
    x = join([x] + got, [place ^ d for d in range(outer)], 1)
    streams = [x[0], x[1]]
    for level in reversed(range(bits - 1)):
        use = [order[level] for order in orders]
        got = [swap(v, 1 << b) for v, b in zip(streams, use)]
        streams = [
            join([v, g], [flag[b], 1 - flag[b]], 0) for v, b, g in zip(streams, use, got)
        ]
    x = jnp.stack(streams)
    return join([x, swap(x, 1)], [flag[0], 1 - flag[0]], 1)


def shards(
    rho_low,
    kprev_low,
    rho_band,
    kprev_band,
    hamiltonian,
    state_site,
    coupling_mag,
    coupling_phase,
    damping_rate,
    low_mode,
    occupation,
    couple_src,
    couple_mode,
    couple_dir,
):
    band_size = lax.axis_size("band")
    own_index = lax.axis_index("band")
    low_count = rho_low.shape[1]
    band_count = rho_band.shape[1]
    size = rho_band.shape[-1]
    sites = coupling_mag.shape[0] // EXPS
    f32 = jnp.float32
    params = functools.partial(pltpu.CompilerParams, vmem_limit_bytes=VMEM_LIMIT)

    shifted = couple_src - low_count
    owner = jnp.where(couple_src >= low_count, shifted // band_count, own_index)
    slot = jnp.where(owner != own_index, shifted % band_count, 0)
    asks = owner[None] == jnp.arange(band_size)[:, None, None]
    wanted = jnp.max(jnp.where(asks, slot[None], 0), axis=(1, 2))
    wanted = jnp.broadcast_to(wanted[:, None, None], (band_size, 1, 128))
    asked = lax.all_to_all(wanted, "band", split_axis=0, concat_axis=0, tiled=True)

    outer = OUTER if band_size % OUTER == 0 else 1
    inner = band_size // outer
    own = jnp.stack([own_index, jnp.int32(band_size), jnp.int32(inner)]).astype(jnp.int32)
    height = size // BLOCKS
    y_band, *send = pl.pallas_call(
        send_kernel,
        in_specs=[smem, smem, vmem, vmem],
        out_specs=[vmem] + [hbm] * (BLOCKS * outer),
        out_shape=[jax.ShapeDtypeStruct((band_count, 2, size, size), f32)]
        + [jax.ShapeDtypeStruct((inner, 2, height, size), f32)] * (BLOCKS * outer),
        scratch_shapes=[pltpu.SemaphoreType.DMA((BLOCKS, band_size))],
        compiler_params=params(),
        name="send",
    )(own, asked, rho_band, kprev_band)

    groups = [[o * inner + p for p in range(inner)] for o in range(outer)]
    received = []
    for block in range(BLOCKS):
        first = send[block * outer : (block + 1) * outer]
        for step in range(1, outer):
            pairs = [(i, i ^ (step * inner)) for i in range(band_size)]
            first[step] = lax.ppermute(first[step], "band", pairs)
        second = jnp.stack(first, axis=1)
        received.append(
            lax.all_to_all(
                second, "band", split_axis=0, concat_axis=0, tiled=True, axis_index_groups=groups
            )
        )

    whole_row = (1, -1)
    ints, flts = pl.pallas_call(
        functools.partial(prep_kernel, low_count),
        in_specs=[smem] + [vmem] * 9,
        out_specs=[vmem, vmem],
        out_shape=[
            jax.ShapeDtypeStruct((8,) + couple_src.shape, jnp.int32),
            jax.ShapeDtypeStruct((7,) + couple_src.shape, f32),
        ],
        name="prep",
    )(
        own,
        couple_src,
        couple_mode,
        couple_dir,
        occupation,
        coupling_mag.reshape(whole_row),
        jnp.cos(coupling_phase).reshape(whole_row),
        jnp.sin(coupling_phase).reshape(whole_row),
        damping_rate.reshape(whole_row),
        low_mode.reshape(whole_row),
    )

    h_re, h_im = hamiltonian[0], hamiltonian[1]
    left = jnp.block([[h_re, -h_im], [h_im, h_re]])
    right = jnp.block([[h_re, h_im], [-h_im, h_re]])
    col, row = state_site[:, None], state_site[None, :]

    turns = -(-low_count // band_size)
    own_op = jnp.minimum(
        own_index + band_size * jnp.arange(turns, dtype=jnp.int32), low_count - 1
    )
    own_block = pl.BlockSpec((2, 1, size, size), lambda g, ops: (0, ops[g], 0, 0))
    top_block = pl.BlockSpec((2, 1, size, size), lambda g, ops: (0, 0, 0, 0))
    partial = pl.pallas_call(
        lambda ops, *refs: low_kernel(*refs),
        grid_spec=pltpu.PrefetchScalarGridSpec(
            num_scalar_prefetch=1,
            grid=(turns,),
            in_specs=[smem] * 2
            + [vmem, own_block, own_block, top_block, top_block]
            + [vmem] * 4,
            out_specs=vmem,
            scratch_shapes=[pltpu.VMEM((sites, size, size), f32)] * 2,
        ),
        out_shape=jax.ShapeDtypeStruct((2, low_count, size, size), f32),
        compiler_params=params(),
        name="low",
    )(
        own_op,
        ints,
        flts,
        y_band,
        rho_low,
        kprev_low,
        rho_low,
        kprev_low,
        left,
        right,
        col,
        row,
    )
    k_low = sum_over_band(partial.reshape(2, -1, size), band_size, outer, own_index)
    k_low = k_low.reshape(partial.shape)

    base = pl.pallas_call(
        local_kernel,
        in_specs=[smem] * 2 + [vmem] * 7,
        out_specs=vmem,
        out_shape=jax.ShapeDtypeStruct((2, band_count, size, size), f32),
        scratch_shapes=[pltpu.VMEM((low_count + band_count, 2, size, size), f32)]
        + [pltpu.VMEM((sites, size, size), f32)] * 2,
        compiler_params=params(),
        name="local",
    )(ints, flts, y_band, rho_low, kprev_low, left, right, col, row)

    k_band = base
    for block in range(BLOCKS):
        rows = pl.BlockSpec(
            (2, band_count, height, size), functools.partial(lambda b, g: (0, 0, b, 0), block)
        )
        k_band = pl.pallas_call(
            far_kernel,
            grid=(1,),
            in_specs=[smem] * 2
            + [
                vmem,
                rows,
                pl.BlockSpec((height, 1), functools.partial(lambda b, g: (b, 0), block)),
                pl.BlockSpec((1, size), lambda g: (0, 0)),
            ],
            out_specs=rows,
            out_shape=jax.ShapeDtypeStruct((2, band_count, size, size), f32),
            scratch_shapes=[pltpu.VMEM((sites, height, size), f32)] * 2,
            input_output_aliases={3: 0},
            compiler_params=params(),
            name=f"far{block}",
        )(ints, flts, received[block], k_band, col, row)
    return (k_low, k_band)


def solution(mesh):
    placed = (
        P(),
        P(),
        P(None, "band", None, None),
        P(None, "band", None, None),
        P(),
        P(),
        P(),
        P(),
        P(),
        P(),
        P("band", None),
        P("band", None),
        P("band", None),
        P("band", None),
    )
    return jax.shard_map(
        shards,
        mesh=mesh,
        in_specs=placed,
        out_specs=(P(), P(None, "band", None, None)),
        check_vma=False,
    )
```

```python
import functools
import math

import jax
import jax.numpy as jnp
from jax import lax
from jax.experimental import pallas as pl
from jax.experimental.pallas import tpu as pltpu
from jax.sharding import PartitionSpec as P


EXPS = 3
OUTER = 4
BLOCKS = (4, 5, 4, 3)
section_weight = 0.2
VMEM_LIMIT = 60 * 1024 * 1024

vmem = pl.BlockSpec(memory_space=pltpu.VMEM)
smem = pl.BlockSpec(memory_space=pltpu.SMEM)
hbm = pl.BlockSpec(memory_space=pl.ANY)


def fill_masks(row_ref, diff_ref, sum_ref=None, start=0):
    sites, height, size = diff_ref.shape
    site_b = jnp.broadcast_to(row_ref[...].astype(jnp.float32), (size, size))
    site_a = jnp.transpose(site_b)[start : start + height]
    site_b = site_b[start : start + height]

    def one_site(s, carry):
        s_f = lax.convert_element_type(s, jnp.float32)
        va = jnp.where(site_a == s_f, 1.0, 0.0)
        vb = jnp.where(site_b == s_f, 1.0, 0.0)
        diff_ref[s] = va - vb
        if sum_ref is not None:
            sum_ref[s] = va + vb
        return carry

    lax.fori_loop(0, sites, one_site, 0)


def split(x):
    high = x.astype(jnp.bfloat16)
    return high, (x - high.astype(jnp.float32)).astype(jnp.bfloat16)


def matmul(x, y):
    def dot(a, b):
        return jnp.dot(a, b, preferred_element_type=jnp.float32)

    return dot(x[0], y[0]) + (dot(x[0], y[1]) + dot(x[1], y[0]))


def commutator(h_re, h_im, y_pair):
    size = y_pair.shape[-1]
    left, right = [], []
    for re, im in zip(h_re, h_im):
        top = jnp.concatenate([re, -im], axis=1)
        low = jnp.concatenate([im, re], axis=1)
        left.append(jnp.concatenate([top, low], axis=0))
        top = jnp.concatenate([re, im], axis=1)
        low = jnp.concatenate([-im, re], axis=1)
        right.append(jnp.concatenate([top, low], axis=0))
    lhs = matmul(left, split(y_pair.reshape(2 * size, size)))
    rhs = matmul(split(jnp.concatenate([y_pair[0], y_pair[1]], axis=1)), right)
    return lhs[:size] - rhs[:, :size], lhs[size:] - rhs[:, size:]


LOW_J, LOW_S, NEAR_M, _, FAR_M, _, COUNTS, OWN_I = range(8)
LOW_A, NEAR_A, _, FAR_A, _, DAMP, OWN_F = range(7)


def prep_kernel(
    low_count, own, src, mode, direction, occ, mag, cos, sin, rate, low_mode, ints, flts
):
    rows, width = src.shape
    modes = occ.shape[1]
    others = low_mode.shape[1]
    own_index, band_size, inner = own[0], own[1], own[2]
    outer = band_size // inner
    f32, i32 = jnp.float32, jnp.int32
    lane_mode = lax.broadcasted_iota(i32, (rows, modes), 1)
    lane_low = lax.broadcasted_iota(i32, (rows, others), 1)
    lane_col = lax.broadcasted_iota(i32, (rows, width), 1)
    occ_f = occ[...].astype(f32)
    mag_b = jnp.broadcast_to(mag[...], (rows, modes))
    cos_b = jnp.broadcast_to(cos[...], (rows, modes))
    sin_b = jnp.broadcast_to(sin[...], (rows, modes))
    rate_b = jnp.broadcast_to(rate[...], (rows, modes))
    mark_b = jnp.broadcast_to(low_mode[...].astype(f32) + 1.0, (rows, others))

    def total(x):
        return jnp.sum(x, axis=1, keepdims=True)

    zero_i = jnp.zeros((rows, width), i32)
    zero_f = jnp.zeros((rows, width), f32)
    int_out = [zero_i] * 6
    flt_out = [zero_f] * 5
    fill = [jnp.zeros((rows, 1), i32)] * 3
    for c in range(width):
        src_c, mode_c = src[:, c : c + 1], mode[:, c : c + 1]
        down = direction[:, c : c + 1] == 1
        hit = lane_mode == mode_c
        level = total(jnp.where(hit, occ_f, 0.0))
        strength = total(jnp.where(hit, mag_b, 0.0))
        amp_down = jnp.sqrt(level * strength)
        amp_up = jnp.sqrt((level + 1.0) * strength)
        alpha = jnp.where(down, amp_down * total(jnp.where(hit, cos_b, 0.0)), amp_up)
        beta = jnp.where(down, amp_down * total(jnp.where(hit, sin_b, 0.0)), 0.0)
        mark = total(jnp.where(lane_low == src_c - 1, mark_b, 0.0))
        held = jnp.where(mark == mode_c.astype(f32) + 1.0, 2.0, 1.0)
        alpha_low = jnp.sqrt(held * strength)
        site = mode_c // EXPS
        live = src_c >= 0
        is_low = live & (src_c < low_count)
        shifted = jnp.maximum(src_c - low_count, 0)
        owner = shifted // rows
        local = is_low | (live & (owner == own_index))
        far_m = (owner % inner) * outer + ((owner // inner) ^ (own_index // inner))
        near_m = jnp.where(is_low, src_c, low_count + shifted % rows)
        lists = (
            (is_low, (src_c, site), (alpha_low,)),
            (local, (near_m, site), (alpha, beta)),
            (live & ~local, (far_m, site), (alpha, beta)),
        )
        at_f = 0
        for which, (flag, int_cols, flt_cols) in enumerate(lists):
            put = (lane_col == fill[which]) & flag
            for i, value in enumerate(int_cols):
                int_out[2 * which + i] = int_out[2 * which + i] + jnp.where(put, value, 0)
            for value in flt_cols:
                flt_out[at_f] = flt_out[at_f] + jnp.where(put, value, 0.0)
                at_f += 1
            fill[which] = fill[which] + jnp.where(flag, 1, 0)
    for i in range(6):
        ints[i] = int_out[i]
    for i in range(5):
        flts[i] = flt_out[i]
    ints[COUNTS] = jnp.where(
        lane_col == 0, fill[0], jnp.where(lane_col == 1, fill[1], fill[2])
    )
    flts[DAMP] = jnp.broadcast_to(total(occ_f * rate_b), (rows, width))
    turn = lax.broadcasted_iota(i32, (rows, 1), 0)
    op = own_index + band_size * turn
    here = jnp.where(op < low_count, 1, 0)
    op = jnp.minimum(op, low_count - 1)
    op_mode = total(jnp.where(lane_low == jnp.maximum(op - 1, 0), mark_b, 0.0)) - 1.0
    op_mode = op_mode.astype(i32)
    hit = lane_mode == op_mode
    raised = jnp.where(op >= 1, 1.0, 0.0)
    amp = jnp.sqrt(total(jnp.where(hit, mag_b, 0.0))) * raised
    amp_cos = amp * total(jnp.where(hit, cos_b, 0.0))
    amp_sin = amp * total(jnp.where(hit, sin_b, 0.0))
    damp = total(jnp.where(hit, rate_b, 0.0)) * raised
    ints[OWN_I] = jnp.where(lane_col == 0, here, jnp.where(lane_col == 1, op_mode // EXPS, op))
    flts[OWN_F] = jnp.where(
        lane_col == 0,
        damp,
        jnp.where(lane_col == 1, amp, jnp.where(lane_col == 2, amp_cos, amp_sin)),
    )


def advance_kernel(rho, kprev, out):
    def advance(i, carry):
        for part in range(2):
            out[i, part] = rho[part, i] + section_weight * kprev[part, i]
        return carry

    lax.fori_loop(0, rho.shape[1], advance, 0)


def send_kernel(first_row, starts, own, asked, y_band, *rest):
    *outs, held, sems, load_sem = rest
    inner = outs[0].shape[0]
    outer = asked.shape[0] // inner
    place = own[0] // inner
    rows = pl.ds(first_row, held.shape[2])
    load = pltpu.make_async_copy(y_band.at[:, :, rows], held, load_sem.at[0])
    load.start()
    load.wait()

    def copy(block, step, p, entry):
        out = outs[block * outer + step]
        rows = pl.ds(starts[block], out.shape[2])
        return pltpu.make_async_copy(
            held.at[entry, :, rows], out.at[p], sems.at[block, step * inner + p]
        )

    for block in range(len(starts)):
        for step in range(outer):

            def start(p, carry):
                copy(block, step, p, asked[(place ^ step) * inner + p, 0, 0]).start()
                return carry

            lax.fori_loop(0, inner, start, 0)
    for block in range(len(starts)):
        for step in range(outer):

            def finish(p, carry):
                copy(block, step, p, 0).wait()
                return carry

            lax.fori_loop(0, inner, finish, 0)


def low_kernel(
    mine, ints, flts, y_band, rho_own, kprev_own, rho_top, kprev_top, ham, row, keep, give, out, diff, sems
):
    size = out.shape[-1]
    step = pl.program_id(0)
    half = size // 2

    @pl.when(step == 0)
    def _():
        fill_masks(row, diff)

        def clear(j, carry):
            out[0, j] = jnp.zeros((size, size), jnp.float32)
            out[1, j] = jnp.zeros((size, size), jnp.float32)
            return carry

        lax.fori_loop(0, out.shape[1], clear, 0)

        def operator(n, carry):
            def term(c, inner):
                j, s, amp = ints[LOW_J, n, c], ints[LOW_S, n, c], flts[LOW_A, n, c]
                for part in range(2):
                    rows = pl.ds(part * half, half)
                    weight = amp * diff[s, rows]
                    out[0, j, rows] += weight * y_band[n, 1, rows]
                    out[1, j, rows] -= weight * y_band[n, 0, rows]
                return inner

            return lax.fori_loop(0, ints[COUNTS, n, 0], term, carry)

        lax.fori_loop(0, y_band.shape[0], operator, 0)

    @pl.when(ints[OWN_I, step, 0] == 1)
    def _():
        s, j = ints[OWN_I, step, 1], ints[OWN_I, step, 2]
        damping, amp, amp_cos, amp_sin = (flts[OWN_F, step, i] for i in range(4))
        own = rho_own[:, 0] + section_weight * kprev_own[:, 0]
        real, imag = commutator(split(ham[0]), split(ham[1]), own)
        top = rho_top[:, 0] + section_weight * kprev_top[:, 0]
        site_b = jnp.broadcast_to(row[...].astype(jnp.float32), (size, size))
        s_f = lax.convert_element_type(s, jnp.float32)
        va = jnp.where(jnp.transpose(site_b) == s_f, 1.0, 0.0)
        vb = jnp.where(site_b == s_f, 1.0, 0.0)
        w_re, w_im = amp_cos * (va - vb), amp_sin * (va + vb)
        out[0, j] += imag - damping * own[0] + (w_re * top[1] + w_im * top[0])
        out[1, j] += -real - damping * own[1] + (w_im * top[1] - w_re * top[0])
        up = amp * (va - vb)
        out[0, 0] += up * own[1]
        out[1, 0] -= up * own[0]

    @pl.when(step == pl.num_programs(0) - 1)
    def _():
        count = keep.shape[1]
        copies = [
            pltpu.make_async_copy(out.at[:, pl.ds(place * count, count)], to, sems.at[i])
            for i, (place, to) in enumerate(((mine[0], keep), (1 - mine[0], give)))
        ]
        for copy in copies:
            copy.start()
        for copy in copies:
            copy.wait()


def add_terms(n, width, rows, which, ints, flts, fetch, diff, summ, start):
    count_at, source_at, alpha_at = which
    together = math.gcd(width, 8)
    at = n * width

    def terms(g, state):
        re, im = state
        for u in range(together):
            c = at + g * together + u
            m, s = ints[source_at, c], ints[source_at + 1, c]
            w_re = flts[alpha_at, c] * diff[s, rows]
            w_im = flts[alpha_at + 1, c] * summ[s, rows]
            y_re, y_im = fetch(m, rows)
            re = re + (w_re * y_im + w_im * y_re)
            im = im + (w_im * y_im - w_re * y_re)
        return re, im

    groups = (ints[COUNTS, at + count_at] + (together - 1)) // together
    return lax.fori_loop(0, groups, terms, start)


def own_kernel(flts, y_band, ham, out):
    h_re, h_im = split(ham[0]), split(ham[1])

    def operator(n, carry):
        y_pair = y_band[n]
        damping = flts[DAMP, n, 0]
        real, imag = commutator(h_re, h_im, y_pair)
        out[0, n] = imag - damping * y_pair[0]
        out[1, n] = -real - damping * y_pair[1]
        return carry

    lax.fori_loop(0, y_band.shape[0], operator, 0)


def near_kernel(ints, flts, y_band, rho_low, kprev_low, base, row, out, pool, diff, summ):
    size = out.shape[-1]
    low_count, band_count = rho_low.shape[1], y_band.shape[0]
    parts = 2
    fill_masks(row, diff, summ)

    def advance(i, carry):
        for part in range(2):
            pool[i, part] = rho_low[part, i] + section_weight * kprev_low[part, i]
        return carry

    lax.fori_loop(0, low_count, advance, 0)

    def keep(i, carry):
        pool[low_count + i] = y_band[i]
        return carry

    lax.fori_loop(0, band_count, keep, 0)

    def operator(n, carry):
        for part in range(parts):
            rows = pl.ds(part * (size // parts), size // parts)
            re, im = add_terms(
                n,
                ints.shape[1] // band_count,
                rows,
                (1, NEAR_M, NEAR_A),
                ints,
                flts,
                lambda m, r: (pool[m, 0, r], pool[m, 1, r]),
                diff,
                summ,
                (base[0, n, rows], base[1, n, rows]),
            )
            out[0, n, rows] = re
            out[1, n, rows] = im
        return carry

    lax.fori_loop(0, band_count, operator, 0)


def far_kernel(start, ints, flts, received, base, row, out, held, diff, summ, sems):
    block = held.shape[2]
    here = pl.ds(start, block)
    fetch = pltpu.make_async_copy(base.at[:, :, here], held, sems.at[0])
    fetch.start()
    fill_masks(row, diff, summ, start)
    fetch.wait()
    rows = pl.ds(0, block)
    last = received.shape[1] - 1
    shift = last.bit_length()

    def operator(n, carry):
        re, im = add_terms(
            n,
            ints.shape[1] // held.shape[1],
            rows,
            (2, FAR_M, FAR_A),
            ints,
            flts,
            lambda m, r: (received[m >> shift, m & last, 0], received[m >> shift, m & last, 1]),
            diff,
            summ,
            (held[0, n], held[1, n]),
        )
        held[0, n] = re
        held[1, n] = im
        return carry

    lax.fori_loop(0, held.shape[1], operator, 0)
    store = pltpu.make_async_copy(held, out.at[:, :, here], sems.at[1])
    store.start()
    store.wait()


def part_of(x, index, parts, axis):
    step = x.shape[axis] // parts
    return lax.dynamic_slice_in_dim(x, index * step, step, axis)


def join(pieces, indices, axis):
    if len(pieces) == 2:
        first, second = pieces
        return jnp.where(
            indices[0] == 0,
            jnp.concatenate([first, second], axis=axis),
            jnp.concatenate([second, first], axis=axis),
        )
    shape = list(pieces[0].shape)
    step = shape[axis]
    shape[axis] *= len(pieces)
    out = jnp.zeros(shape, pieces[0].dtype)
    for piece, index in zip(pieces, indices):
        out = lax.dynamic_update_slice_in_dim(out, piece, index * step, axis)
    return out


def sum_over_band(keep, give, band_size, outer, own_index):
    inner = band_size // outer
    bits = inner.bit_length() - 1
    place = own_index // inner
    flag = [(own_index >> b) & 1 for b in range(bits)]
    plain = list(range(1, bits))
    orders = (plain, plain[:2][::-1] + plain[2:])

    def swap(value, distance):
        pairs = [(i, i ^ distance) for i in range(band_size)]
        return lax.ppermute(value, "band", pairs)

    x = keep + swap(give, 1)
    streams = [x[0], x[1]]
    for level in range(bits - 1):
        use = [order[level] for order in orders]
        got = [swap(part_of(v, 1 - flag[b], 2, 0), 1 << b) for v, b in zip(streams, use)]
        streams = [part_of(v, flag[b], 2, 0) + g for v, b, g in zip(streams, use, got)]
    x = jnp.stack(streams)
    got = [swap(part_of(x, place ^ d, outer, 1), d * inner) for d in range(1, outer)]
    x = part_of(x, place, outer, 1)
    for other in got:
        x = x + other
    got = [swap(x, d * inner) for d in range(1, outer)]
    x = join([x] + got, [place ^ d for d in range(outer)], 1)
    streams = [x[0], x[1]]
    for level in reversed(range(bits - 1)):
        use = [order[level] for order in orders]
        got = [swap(v, 1 << b) for v, b in zip(streams, use)]
        streams = [
            join([v, g], [flag[b], 1 - flag[b]], 0) for v, b, g in zip(streams, use, got)
        ]
    x = jnp.stack(streams)
    got = swap(x, 1)
    return join([x, got], [flag[0], 1 - flag[0]], 1)


def shards(
    rho_low,
    kprev_low,
    rho_band,
    kprev_band,
    hamiltonian,
    state_site,
    coupling_mag,
    coupling_phase,
    damping_rate,
    low_mode,
    occupation,
    couple_src,
    couple_mode,
    couple_dir,
):
    band_size = lax.axis_size("band")
    own_index = lax.axis_index("band")
    low_count = rho_low.shape[1]
    band_count = rho_band.shape[1]
    size = rho_band.shape[-1]
    sites = coupling_mag.shape[0] // EXPS
    f32 = jnp.float32
    params = functools.partial(pltpu.CompilerParams, vmem_limit_bytes=VMEM_LIMIT)

    shifted = couple_src - low_count
    owner = jnp.where(couple_src >= low_count, shifted // band_count, own_index)
    slot = jnp.where(owner != own_index, shifted % band_count, 0)
    asks = owner[None] == jnp.arange(band_size)[:, None, None]
    wanted = jnp.max(jnp.where(asks, slot[None], 0), axis=(1, 2))
    wanted = jnp.broadcast_to(wanted[:, None, None], (band_size, 1, 128))
    asked = lax.all_to_all(wanted, "band", split_axis=0, concat_axis=0, tiled=True)

    outer = OUTER if band_size % OUTER == 0 else 1
    inner = band_size // outer
    own = jnp.stack([own_index, jnp.int32(band_size), jnp.int32(inner)]).astype(jnp.int32)
    heights = [size * part // sum(BLOCKS) for part in BLOCKS]
    starts = [sum(heights[:i]) for i in range(len(heights))]
    y_band = pl.pallas_call(
        advance_kernel,
        in_specs=[vmem, vmem],
        out_specs=vmem,
        out_shape=jax.ShapeDtypeStruct((band_count, 2, size, size), f32),
        compiler_params=params(),
        name="advance",
    )(rho_band, kprev_band)
    send = []
    for which in (slice(0, 1), slice(1, None)):
        first_row, last_row = starts[which][0], starts[which][-1] + heights[which][-1]
        send += pl.pallas_call(
            functools.partial(send_kernel, first_row, [start - first_row for start in starts[which]]),
            in_specs=[smem, smem, hbm],
            out_specs=[hbm] * (len(starts[which]) * outer),
            out_shape=[
                jax.ShapeDtypeStruct((inner, 2, height, size), f32)
                for height in heights[which]
                for _ in range(outer)
            ],
            scratch_shapes=[
                pltpu.VMEM((band_count, 2, last_row - first_row, size), f32),
                pltpu.SemaphoreType.DMA((len(starts[which]), band_size)),
                pltpu.SemaphoreType.DMA((1,)),
            ],
            compiler_params=params(),
        )(own, asked, y_band)

    groups = [[o * inner + p for p in range(inner)] for o in range(outer)]
    received = []
    for block in range(len(starts)):
        first = list(send[block * outer : (block + 1) * outer])
        for step in range(1, outer):
            pairs = [(i, i ^ (step * inner)) for i in range(band_size)]
            first[step] = lax.ppermute(first[step], "band", pairs)
        second = jnp.stack(first, axis=1)
        received.append(
            lax.all_to_all(
                second,
                "band",
                split_axis=0,
                concat_axis=0,
                tiled=True,
                axis_index_groups=groups,
            )
        )

    whole_row = (1, -1)
    ints, flts = pl.pallas_call(
        functools.partial(prep_kernel, low_count),
        in_specs=[smem] + [vmem] * 9,
        out_specs=[vmem, vmem],
        out_shape=[
            jax.ShapeDtypeStruct((8,) + couple_src.shape, jnp.int32),
            jax.ShapeDtypeStruct((7,) + couple_src.shape, f32),
        ],
        name="prep",
    )(
        own,
        couple_src,
        couple_mode,
        couple_dir,
        occupation,
        coupling_mag.reshape(whole_row),
        jnp.cos(coupling_phase).reshape(whole_row),
        jnp.sin(coupling_phase).reshape(whole_row),
        damping_rate.reshape(whole_row),
        low_mode.reshape(whole_row),
    )

    row = state_site[None, :]

    ints_flat, flts_flat = ints.reshape(8, -1), flts.reshape(7, -1)

    turns = -(-low_count // band_size)
    own_op = jnp.minimum(
        own_index + band_size * jnp.arange(turns, dtype=jnp.int32), low_count - 1
    )
    own_block = pl.BlockSpec((2, 1, size, size), lambda g, ops: (0, ops[g], 0, 0))
    top_block = pl.BlockSpec((2, 1, size, size), lambda g, ops: (0, 0, 0, 0))
    half_shape = (2, low_count // 2, size, size)
    keep, give = pl.pallas_call(
        lambda ops, *refs: low_kernel(*refs),
        grid_spec=pltpu.PrefetchScalarGridSpec(
            num_scalar_prefetch=1,
            grid=(turns,),
            in_specs=[smem] * 3
            + [vmem, own_block, own_block, top_block, top_block]
            + [vmem] * 2,
            out_specs=[hbm] * 2,
            scratch_shapes=[
                pltpu.VMEM((2, low_count, size, size), f32),
                pltpu.VMEM((sites, size, size), f32),
                pltpu.SemaphoreType.DMA((2,)),
            ],
        ),
        out_shape=[jax.ShapeDtypeStruct(half_shape, f32)] * 2,
        compiler_params=params(),
        name="low",
    )(
        own_op,
        (own_index & 1).astype(jnp.int32)[None],
        ints,
        flts,
        y_band,
        rho_low,
        kprev_low,
        rho_low,
        kprev_low,
        hamiltonian,
        row,
    )
    flat = (2, -1, size)
    k_low = sum_over_band(keep.reshape(flat), give.reshape(flat), band_size, outer, own_index)
    k_low = k_low.reshape(rho_low.shape)

    base = pl.pallas_call(
        own_kernel,
        in_specs=[smem] + [vmem] * 2,
        out_specs=vmem,
        out_shape=jax.ShapeDtypeStruct((2, band_count, size, size), f32),
        compiler_params=params(),
        name="own",
    )(flts, y_band, hamiltonian)
    base = pl.pallas_call(
        near_kernel,
        in_specs=[smem] * 2 + [vmem] * 5,
        out_specs=vmem,
        out_shape=jax.ShapeDtypeStruct((2, band_count, size, size), f32),
        scratch_shapes=[pltpu.VMEM((low_count + band_count, 2, size, size), f32)]
        + [pltpu.VMEM((sites, size, size), f32)] * 2,
        compiler_params=params(),
        name="near",
    )(ints_flat, flts_flat, y_band, rho_low, kprev_low, base, row)

    k_band = base
    for block, (start, height) in enumerate(zip(starts, heights)):
        k_band = pl.pallas_call(
            functools.partial(far_kernel, start),
            in_specs=[smem] * 2 + [vmem, hbm, vmem],
            out_specs=hbm,
            out_shape=jax.ShapeDtypeStruct((2, band_count, size, size), f32),
            scratch_shapes=[pltpu.VMEM((2, band_count, height, size), f32)]
            + [pltpu.VMEM((sites, height, size), f32)] * 2
            + [pltpu.SemaphoreType.DMA((2,))],
            input_output_aliases={3: 0},
            compiler_params=params(),
        )(ints_flat, flts_flat, received[block], k_band, row)
    return (k_low, k_band)


def solution(mesh):
    placed = (
        P(),
        P(),
        P(None, "band", None, None),
        P(None, "band", None, None),
        P(),
        P(),
        P(),
        P(),
        P(),
        P(),
        P("band", None),
        P("band", None),
        P("band", None),
        P("band", None),
    )
    return jax.shard_map(
        shards,
        mesh=mesh,
        in_specs=placed,
        out_specs=(P(), P(None, "band", None, None)),
        check_vma=False,
    )
```

```python
import functools
import math

import jax
import jax.numpy as jnp
from jax import lax
from jax.experimental import pallas as pl
from jax.experimental.pallas import tpu as pltpu
from jax.sharding import PartitionSpec as P


EXPS = 3
OUTER = 4
BLOCKS = (4, 5, 7)
section_weight = 0.2
VMEM_LIMIT = 60 * 1024 * 1024

vmem = pl.BlockSpec(memory_space=pltpu.VMEM)
smem = pl.BlockSpec(memory_space=pltpu.SMEM)
hbm = pl.BlockSpec(memory_space=pl.ANY)


def fill_masks(row_ref, diff_ref, sum_ref=None, start=0):
    sites, height, size = diff_ref.shape
    site_b = jnp.broadcast_to(row_ref[...].astype(jnp.float32), (size, size))
    site_a = jnp.transpose(site_b)[start : start + height]
    site_b = site_b[start : start + height]

    def one_site(s, carry):
        s_f = lax.convert_element_type(s, jnp.float32)
        va = jnp.where(site_a == s_f, 1.0, 0.0)
        vb = jnp.where(site_b == s_f, 1.0, 0.0)
        diff_ref[s] = va - vb
        if sum_ref is not None:
            sum_ref[s] = va + vb
        return carry

    lax.fori_loop(0, sites, one_site, 0)


def split(x):
    high = x.astype(jnp.bfloat16)
    return high, (x - high.astype(jnp.float32)).astype(jnp.bfloat16)


def matmul(x, y):
    def dot(a, b):
        return jnp.dot(a, b, preferred_element_type=jnp.float32)

    return dot(x[0], y[0]) + (dot(x[0], y[1]) + dot(x[1], y[0]))


def commutator(h_re, h_im, y_pair):
    size = y_pair.shape[-1]
    left, right = [], []
    for re, im in zip(h_re, h_im):
        top = jnp.concatenate([re, -im], axis=1)
        low = jnp.concatenate([im, re], axis=1)
        left.append(jnp.concatenate([top, low], axis=0))
        top = jnp.concatenate([re, im], axis=1)
        low = jnp.concatenate([-im, re], axis=1)
        right.append(jnp.concatenate([top, low], axis=0))
    lhs = matmul(left, split(y_pair.reshape(2 * size, size)))
    rhs = matmul(split(jnp.concatenate([y_pair[0], y_pair[1]], axis=1)), right)
    return lhs[:size] - rhs[:, :size], lhs[size:] - rhs[:, size:]


LOW_J, LOW_S, NEAR_M, _, FAR_M, _, COUNTS, OWN_I = range(8)
LOW_A, NEAR_A, _, FAR_A, _, DAMP, OWN_F = range(7)


def prep_kernel(
    low_count, own, src, mode, direction, occ, mag, cos, sin, rate, low_mode, ints, flts
):
    rows, width = src.shape
    modes = occ.shape[1]
    others = low_mode.shape[1]
    own_index, band_size, inner = own[0], own[1], own[2]
    outer = band_size // inner
    f32, i32 = jnp.float32, jnp.int32
    lane_mode = lax.broadcasted_iota(i32, (rows, modes), 1)
    lane_low = lax.broadcasted_iota(i32, (rows, others), 1)
    lane_col = lax.broadcasted_iota(i32, (rows, width), 1)
    occ_f = occ[...].astype(f32)
    mag_b = jnp.broadcast_to(mag[...], (rows, modes))
    cos_b = jnp.broadcast_to(cos[...], (rows, modes))
    sin_b = jnp.broadcast_to(sin[...], (rows, modes))
    rate_b = jnp.broadcast_to(rate[...], (rows, modes))
    mark_b = jnp.broadcast_to(low_mode[...].astype(f32) + 1.0, (rows, others))

    def total(x):
        return jnp.sum(x, axis=1, keepdims=True)

    zero_i = jnp.zeros((rows, width), i32)
    zero_f = jnp.zeros((rows, width), f32)
    int_out = [zero_i] * 6
    flt_out = [zero_f] * 5
    fill = [jnp.zeros((rows, 1), i32)] * 3
    for c in range(width):
        src_c, mode_c = src[:, c : c + 1], mode[:, c : c + 1]
        down = direction[:, c : c + 1] == 1
        hit = lane_mode == mode_c
        level = total(jnp.where(hit, occ_f, 0.0))
        strength = total(jnp.where(hit, mag_b, 0.0))
        amp_down = jnp.sqrt(level * strength)
        amp_up = jnp.sqrt((level + 1.0) * strength)
        alpha = jnp.where(down, amp_down * total(jnp.where(hit, cos_b, 0.0)), amp_up)
        beta = jnp.where(down, amp_down * total(jnp.where(hit, sin_b, 0.0)), 0.0)
        mark = total(jnp.where(lane_low == src_c - 1, mark_b, 0.0))
        held = jnp.where(mark == mode_c.astype(f32) + 1.0, 2.0, 1.0)
        alpha_low = jnp.sqrt(held * strength)
        site = mode_c // EXPS
        live = src_c >= 0
        is_low = live & (src_c < low_count)
        shifted = jnp.maximum(src_c - low_count, 0)
        owner = shifted // rows
        local = is_low | (live & (owner == own_index))
        far_m = (owner % inner) * outer + ((owner // inner) ^ (own_index // inner))
        near_m = jnp.where(is_low, src_c, low_count + shifted % rows)
        lists = (
            (is_low, (src_c, site), (alpha_low,)),
            (local, (near_m, site), (alpha, beta)),
            (live & ~local, (far_m, site), (alpha, beta)),
        )
        at_f = 0
        for which, (flag, int_cols, flt_cols) in enumerate(lists):
            put = (lane_col == fill[which]) & flag
            for i, value in enumerate(int_cols):
                int_out[2 * which + i] = int_out[2 * which + i] + jnp.where(put, value, 0)
            for value in flt_cols:
                flt_out[at_f] = flt_out[at_f] + jnp.where(put, value, 0.0)
                at_f += 1
            fill[which] = fill[which] + jnp.where(flag, 1, 0)
    for i in range(6):
        ints[i] = int_out[i]
    for i in range(5):
        flts[i] = flt_out[i]
    ints[COUNTS] = jnp.where(
        lane_col == 0, fill[0], jnp.where(lane_col == 1, fill[1], fill[2])
    )
    flts[DAMP] = jnp.broadcast_to(total(occ_f * rate_b), (rows, width))
    turn = lax.broadcasted_iota(i32, (rows, 1), 0)
    op = own_index + band_size * turn
    here = jnp.where(op < low_count, 1, 0)
    op = jnp.minimum(op, low_count - 1)
    op_mode = total(jnp.where(lane_low == jnp.maximum(op - 1, 0), mark_b, 0.0)) - 1.0
    op_mode = op_mode.astype(i32)
    hit = lane_mode == op_mode
    raised = jnp.where(op >= 1, 1.0, 0.0)
    amp = jnp.sqrt(total(jnp.where(hit, mag_b, 0.0))) * raised
    amp_cos = amp * total(jnp.where(hit, cos_b, 0.0))
    amp_sin = amp * total(jnp.where(hit, sin_b, 0.0))
    damp = total(jnp.where(hit, rate_b, 0.0)) * raised
    ints[OWN_I] = jnp.where(lane_col == 0, here, jnp.where(lane_col == 1, op_mode // EXPS, op))
    flts[OWN_F] = jnp.where(
        lane_col == 0,
        damp,
        jnp.where(lane_col == 1, amp, jnp.where(lane_col == 2, amp_cos, amp_sin)),
    )


def advance_kernel(rho, kprev, out):
    def advance(i, carry):
        for part in range(2):
            out[i, part] = rho[part, i] + section_weight * kprev[part, i]
        return carry

    lax.fori_loop(0, rho.shape[1], advance, 0)


def send_kernel(first_row, blocks, own, asked, y_band, *rest):
    *outs, held, sems, load_sem = rest
    rows = pl.ds(first_row, held.shape[2])
    load = pltpu.make_async_copy(y_band.at[:, :, rows], held, load_sem.at[0])
    load.start()
    load.wait()

    def copies(i, act):
        out_at = 0
        for at, (start, height, steps, inner) in enumerate(blocks):
            place = own[0] // inner
            many = len(outs[out_at].shape) == 4
            for step in range(steps):
                out = outs[out_at + step] if many else outs[out_at].at[:, step]

                def one(p, carry):
                    entry = asked[(place ^ step) * inner + p, 0, 0] if i == 0 else 0
                    act(
                        pltpu.make_async_copy(
                            held.at[entry, :, pl.ds(start, height)],
                            out.at[p],
                            sems.at[at, step * inner + p],
                        )
                    )
                    return carry

                lax.fori_loop(0, inner, one, 0)
            out_at += steps if many else 1

    copies(0, lambda copy: copy.start())
    copies(1, lambda copy: copy.wait())


def low_kernel(
    mine, ints, flts, y_band, rho_own, kprev_own, rho_top, kprev_top, ham, row, keep, give, out, diff, sems
):
    size = out.shape[-1]
    step = pl.program_id(0)
    half = size // 2

    @pl.when(step == 0)
    def _():
        fill_masks(row, diff)

        def clear(j, carry):
            out[0, j] = jnp.zeros((size, size), jnp.float32)
            out[1, j] = jnp.zeros((size, size), jnp.float32)
            return carry

        lax.fori_loop(0, out.shape[1], clear, 0)

        def operator(n, carry):
            def term(c, inner):
                j, s, amp = ints[LOW_J, n, c], ints[LOW_S, n, c], flts[LOW_A, n, c]
                for part in range(2):
                    rows = pl.ds(part * half, half)
                    weight = amp * diff[s, rows]
                    out[0, j, rows] += weight * y_band[n, 1, rows]
                    out[1, j, rows] -= weight * y_band[n, 0, rows]
                return inner

            return lax.fori_loop(0, ints[COUNTS, n, 0], term, carry)

        lax.fori_loop(0, y_band.shape[0], operator, 0)

    @pl.when(ints[OWN_I, step, 0] == 1)
    def _():
        s, j = ints[OWN_I, step, 1], ints[OWN_I, step, 2]
        damping, amp, amp_cos, amp_sin = (flts[OWN_F, step, i] for i in range(4))
        own = rho_own[:, 0] + section_weight * kprev_own[:, 0]
        real, imag = commutator(split(ham[0]), split(ham[1]), own)
        top = rho_top[:, 0] + section_weight * kprev_top[:, 0]
        site_b = jnp.broadcast_to(row[...].astype(jnp.float32), (size, size))
        s_f = lax.convert_element_type(s, jnp.float32)
        va = jnp.where(jnp.transpose(site_b) == s_f, 1.0, 0.0)
        vb = jnp.where(site_b == s_f, 1.0, 0.0)
        w_re, w_im = amp_cos * (va - vb), amp_sin * (va + vb)
        out[0, j] += imag - damping * own[0] + (w_re * top[1] + w_im * top[0])
        out[1, j] += -real - damping * own[1] + (w_im * top[1] - w_re * top[0])
        up = amp * (va - vb)
        out[0, 0] += up * own[1]
        out[1, 0] -= up * own[0]

    @pl.when(step == pl.num_programs(0) - 1)
    def _():
        count = keep.shape[1]
        copies = [
            pltpu.make_async_copy(out.at[:, pl.ds(place * count, count)], to, sems.at[i])
            for i, (place, to) in enumerate(((mine[0], keep), (1 - mine[0], give)))
        ]
        for copy in copies:
            copy.start()
        for copy in copies:
            copy.wait()


def add_terms(n, width, rows, which, ints, flts, fetch, diff, summ, start):
    count_at, source_at, alpha_at = which
    together = math.gcd(width, 8)
    at = n * width

    def terms(g, state):
        re, im = state
        for u in range(together):
            c = at + g * together + u
            m, s = ints[source_at, c], ints[source_at + 1, c]
            w_re = flts[alpha_at, c] * diff[s, rows]
            w_im = flts[alpha_at + 1, c] * summ[s, rows]
            y_re, y_im = fetch(m, rows)
            re = re + (w_re * y_im + w_im * y_re)
            im = im + (w_im * y_im - w_re * y_re)
        return re, im

    groups = (ints[COUNTS, at + count_at] + (together - 1)) // together
    return lax.fori_loop(0, groups, terms, start)


def own_kernel(flts, y_band, ham, out):
    h_re, h_im = split(ham[0]), split(ham[1])

    def operator(n, carry):
        y_pair = y_band[n]
        damping = flts[DAMP, n, 0]
        real, imag = commutator(h_re, h_im, y_pair)
        out[0, n] = imag - damping * y_pair[0]
        out[1, n] = -real - damping * y_pair[1]
        return carry

    lax.fori_loop(0, y_band.shape[0], operator, 0)


def near_kernel(ints, flts, y_band, rho_low, kprev_low, base, row, out, pool, diff, summ):
    size = out.shape[-1]
    low_count, band_count = rho_low.shape[1], y_band.shape[0]
    parts = 2
    fill_masks(row, diff, summ)

    def advance(i, carry):
        for part in range(2):
            pool[i, part] = rho_low[part, i] + section_weight * kprev_low[part, i]
        return carry

    lax.fori_loop(0, low_count, advance, 0)

    def keep(i, carry):
        pool[low_count + i] = y_band[i]
        return carry

    lax.fori_loop(0, band_count, keep, 0)

    def operator(n, carry):
        for part in range(parts):
            rows = pl.ds(part * (size // parts), size // parts)
            re, im = add_terms(
                n,
                ints.shape[1] // band_count,
                rows,
                (1, NEAR_M, NEAR_A),
                ints,
                flts,
                lambda m, r: (pool[m, 0, r], pool[m, 1, r]),
                diff,
                summ,
                (base[0, n, rows], base[1, n, rows]),
            )
            out[0, n, rows] = re
            out[1, n, rows] = im
        return carry

    lax.fori_loop(0, band_count, operator, 0)


def far_kernel(start, ints, flts, base, row, *rest):
    *parts, out, held, received, diff, summ, sems = rest
    block = held.shape[2]
    here = pl.ds(start, block)
    loads = [pltpu.make_async_copy(base.at[:, :, here], held, sems.at[0])]
    if len(parts) == 1:
        loads.append(pltpu.make_async_copy(parts[0], received, sems.at[1]))
    else:
        for step, part in enumerate(parts):
            source = part if step else part.at[:, 0]
            loads.append(pltpu.make_async_copy(source, received.at[:, step], sems.at[1 + step]))
    for load in loads:
        load.start()
    fill_masks(row, diff, summ, start)
    for load in loads:
        load.wait()
    rows = pl.ds(0, block)
    last = received.shape[1] - 1
    shift = last.bit_length()

    def operator(n, carry):
        re, im = add_terms(
            n,
            ints.shape[1] // held.shape[1],
            rows,
            (2, FAR_M, FAR_A),
            ints,
            flts,
            lambda m, r: (received[m >> shift, m & last, 0], received[m >> shift, m & last, 1]),
            diff,
            summ,
            (held[0, n], held[1, n]),
        )
        held[0, n] = re
        held[1, n] = im
        return carry

    lax.fori_loop(0, held.shape[1], operator, 0)
    store = pltpu.make_async_copy(held, out.at[:, :, here], sems.at[0])
    store.start()
    store.wait()


def part_of(x, index, parts, axis):
    step = x.shape[axis] // parts
    return lax.dynamic_slice_in_dim(x, index * step, step, axis)


def join(pieces, indices, axis):
    if len(pieces) == 2:
        first, second = pieces
        return jnp.where(
            indices[0] == 0,
            jnp.concatenate([first, second], axis=axis),
            jnp.concatenate([second, first], axis=axis),
        )
    shape = list(pieces[0].shape)
    step = shape[axis]
    shape[axis] *= len(pieces)
    out = jnp.zeros(shape, pieces[0].dtype)
    for piece, index in zip(pieces, indices):
        out = lax.dynamic_update_slice_in_dim(out, piece, index * step, axis)
    return out


def lay_kernel(places, *refs):
    *pieces, out, sems = refs
    count = pieces[0].shape[0]
    copies = []
    for i, piece in enumerate(pieces):
        core, axis, stream = i // 4, (i // 2) % 2, i % 2
        half = places[0] if core == 0 else 1 - places[0]
        quarter = places[1 + stream] if axis == 0 else 1 - places[1 + stream]
        start = pl.multiple_of((2 * half + quarter) * count, count)
        copies.append(
            pltpu.make_async_copy(piece, out.at[stream, pl.ds(start, count)], sems.at[i])
        )
    for copy in copies:
        copy.start()
    for copy in copies:
        copy.wait()


def sum_over_band(keep, give, band_size, outer, own_index):
    inner = band_size // outer
    bits = inner.bit_length() - 1
    place = own_index // inner
    flag = [(own_index >> b) & 1 for b in range(bits)]
    plain = list(range(1, bits))
    orders = (plain, plain[:2][::-1] + plain[2:])

    def swap(value, distance):
        pairs = [(i, i ^ distance) for i in range(band_size)]
        return lax.ppermute(value, "band", pairs)

    x = keep + swap(give, 1)
    streams = [x[0], x[1]]
    for level in range(bits - 1):
        use = [order[level] for order in orders]
        got = [swap(part_of(v, 1 - flag[b], 2, 0), 1 << b) for v, b in zip(streams, use)]
        streams = [part_of(v, flag[b], 2, 0) + g for v, b, g in zip(streams, use, got)]
    x = jnp.stack(streams)
    got = [swap(part_of(x, place ^ d, outer, 1), d * inner) for d in range(1, outer)]
    x = part_of(x, place, outer, 1)
    for other in got:
        x = x + other
    got = [swap(x, d * inner) for d in range(1, outer)]
    x = join([x] + got, [place ^ d for d in range(outer)], 1)
    streams = [x[0], x[1]]
    for level in reversed(range(1, bits - 1)):
        use = [order[level] for order in orders]
        got = [swap(v, 1 << b) for v, b in zip(streams, use)]
        streams = [
            join([v, g], [flag[b], 1 - flag[b]], 0) for v, b, g in zip(streams, use, got)
        ]
    use = [order[0] for order in orders]
    got = [swap(v, 1 << b) for v, b in zip(streams, use)]
    pieces = streams + got
    pieces += [swap(piece, 1) for piece in pieces]
    places = jnp.stack([flag[0]] + [flag[b] for b in use]).astype(jnp.int32)
    count, width = pieces[0].shape
    return pl.pallas_call(
        lay_kernel,
        in_specs=[smem] + [vmem] * 8,
        out_specs=hbm,
        out_shape=jax.ShapeDtypeStruct((2, 4 * count, width), jnp.float32),
        scratch_shapes=[pltpu.SemaphoreType.DMA((8,))],
        compiler_params=pltpu.CompilerParams(vmem_limit_bytes=VMEM_LIMIT),
        name="lay",
    )(places, *pieces)


def shards(
    rho_low,
    kprev_low,
    rho_band,
    kprev_band,
    hamiltonian,
    state_site,
    coupling_mag,
    coupling_phase,
    damping_rate,
    low_mode,
    occupation,
    couple_src,
    couple_mode,
    couple_dir,
):
    band_size = lax.axis_size("band")
    own_index = lax.axis_index("band")
    low_count = rho_low.shape[1]
    band_count = rho_band.shape[1]
    size = rho_band.shape[-1]
    sites = coupling_mag.shape[0] // EXPS
    f32 = jnp.float32
    params = functools.partial(pltpu.CompilerParams, vmem_limit_bytes=VMEM_LIMIT)

    shifted = couple_src - low_count
    owner = jnp.where(couple_src >= low_count, shifted // band_count, own_index)
    slot = jnp.where(owner != own_index, shifted % band_count, 0)
    asks = owner[None] == jnp.arange(band_size)[:, None, None]
    wanted = jnp.max(jnp.where(asks, slot[None], 0), axis=(1, 2))
    wanted = jnp.broadcast_to(wanted[:, None, None], (band_size, 1, 128))
    asked = lax.all_to_all(wanted, "band", split_axis=0, concat_axis=0, tiled=True)

    outer = OUTER if band_size % OUTER == 0 else 1
    inner = band_size // outer
    own = jnp.stack([own_index, jnp.int32(band_size), jnp.int32(inner)]).astype(jnp.int32)
    heights = [size * part // sum(BLOCKS) for part in BLOCKS]
    starts = [sum(heights[:i]) for i in range(len(heights))]
    y_band = pl.pallas_call(
        advance_kernel,
        in_specs=[vmem, vmem],
        out_specs=vmem,
        out_shape=jax.ShapeDtypeStruct((band_count, 2, size, size), f32),
        compiler_params=params(),
        name="advance",
    )(rho_band, kprev_band)
    last = len(starts) - 1
    send = []
    for which in (slice(0, 1), slice(1, None)):
        first_row, last_row = starts[which][0], starts[which][-1] + heights[which][-1]
        shapes = []
        for height in heights[which][: None if which.start == 0 else -1]:
            shapes += [(inner, 2, height, size)] * outer
        if which.start:
            shapes.append((inner, outer, 2, heights[last], size))
        send += pl.pallas_call(
            functools.partial(
                send_kernel,
                first_row,
                [(s - first_row, h, outer, inner) for s, h in zip(starts[which], heights[which])],
            ),
            in_specs=[smem, smem, hbm],
            out_specs=[hbm] * len(shapes),
            out_shape=[jax.ShapeDtypeStruct(shape, f32) for shape in shapes],
            scratch_shapes=[
                pltpu.VMEM((band_count, 2, last_row - first_row, size), f32),
                pltpu.SemaphoreType.DMA((len(starts[which]), band_size)),
                pltpu.SemaphoreType.DMA((1,)),
            ],
            compiler_params=params(),
        )(own, asked, y_band)

    groups = [[o * inner + p for p in range(inner)] for o in range(outer)]

    def go_out(value, step):
        pairs = [(i, i ^ (step * inner)) for i in range(band_size)]
        return lax.ppermute(value, "band", pairs)

    def go_in(value):
        return lax.all_to_all(
            value, "band", split_axis=0, concat_axis=0, tiled=True, axis_index_groups=groups
        )

    received = []
    for block in range(last):
        first = send[block * outer : (block + 1) * outer]
        moved = [first[0]] + [go_out(first[step], step) for step in range(1, outer)]
        received.append([go_in(jnp.stack(moved, axis=1))])
    first = go_in(send[-1])
    received.append([first] + [go_out(first[:, step], step) for step in range(1, outer)])

    whole_row = (1, -1)
    ints, flts = pl.pallas_call(
        functools.partial(prep_kernel, low_count),
        in_specs=[smem] + [vmem] * 9,
        out_specs=[vmem, vmem],
        out_shape=[
            jax.ShapeDtypeStruct((8,) + couple_src.shape, jnp.int32),
            jax.ShapeDtypeStruct((7,) + couple_src.shape, f32),
        ],
        name="prep",
    )(
        own,
        couple_src,
        couple_mode,
        couple_dir,
        occupation,
        coupling_mag.reshape(whole_row),
        jnp.cos(coupling_phase).reshape(whole_row),
        jnp.sin(coupling_phase).reshape(whole_row),
        damping_rate.reshape(whole_row),
        low_mode.reshape(whole_row),
    )

    row = state_site[None, :]

    ints_flat, flts_flat = ints.reshape(8, -1), flts.reshape(7, -1)

    turns = -(-low_count // band_size)
    own_op = jnp.minimum(
        own_index + band_size * jnp.arange(turns, dtype=jnp.int32), low_count - 1
    )
    own_block = pl.BlockSpec((2, 1, size, size), lambda g, ops: (0, ops[g], 0, 0))
    top_block = pl.BlockSpec((2, 1, size, size), lambda g, ops: (0, 0, 0, 0))
    half_shape = (2, low_count // 2, size, size)
    keep, give = pl.pallas_call(
        lambda ops, *refs: low_kernel(*refs),
        grid_spec=pltpu.PrefetchScalarGridSpec(
            num_scalar_prefetch=1,
            grid=(turns,),
            in_specs=[smem] * 3
            + [vmem, own_block, own_block, top_block, top_block]
            + [vmem] * 2,
            out_specs=[hbm] * 2,
            scratch_shapes=[
                pltpu.VMEM((2, low_count, size, size), f32),
                pltpu.VMEM((sites, size, size), f32),
                pltpu.SemaphoreType.DMA((2,)),
            ],
        ),
        out_shape=[jax.ShapeDtypeStruct(half_shape, f32)] * 2,
        compiler_params=params(),
        name="low",
    )(
        own_op,
        (own_index & 1).astype(jnp.int32)[None],
        ints,
        flts,
        y_band,
        rho_low,
        kprev_low,
        rho_low,
        kprev_low,
        hamiltonian,
        row,
    )
    flat = (2, -1, size)
    k_low = sum_over_band(keep.reshape(flat), give.reshape(flat), band_size, outer, own_index)
    k_low = k_low.reshape(rho_low.shape)

    base = pl.pallas_call(
        own_kernel,
        in_specs=[smem] + [vmem] * 2,
        out_specs=vmem,
        out_shape=jax.ShapeDtypeStruct((2, band_count, size, size), f32),
        compiler_params=params(),
        name="own",
    )(flts, y_band, hamiltonian)

    def far_terms(k_band, block):
        height = heights[block]
        parts = received[block]
        return pl.pallas_call(
            functools.partial(far_kernel, starts[block]),
            in_specs=[smem] * 2 + [hbm, vmem] + [hbm] * len(parts),
            out_specs=hbm,
            out_shape=jax.ShapeDtypeStruct((2, band_count, size, size), f32),
            scratch_shapes=[pltpu.VMEM((2, band_count, height, size), f32)]
            + [pltpu.VMEM((inner, outer, 2, height, size), f32)]
            + [pltpu.VMEM((sites, height, size), f32)] * 2
            + [pltpu.SemaphoreType.DMA((1 + len(parts),))],
            input_output_aliases={2: 0},
            compiler_params=params(),
        )(ints_flat, flts_flat, k_band, row, *parts)

    k_band = base
    for block in range(last):
        k_band = far_terms(k_band, block)
    k_band = pl.pallas_call(
        near_kernel,
        in_specs=[smem] * 2 + [vmem] * 5,
        out_specs=vmem,
        out_shape=jax.ShapeDtypeStruct((2, band_count, size, size), f32),
        scratch_shapes=[pltpu.VMEM((low_count + band_count, 2, size, size), f32)]
        + [pltpu.VMEM((sites, size, size), f32)] * 2,
        compiler_params=params(),
        name="near",
    )(ints_flat, flts_flat, y_band, rho_low, kprev_low, k_band, row)
    k_band = far_terms(k_band, last)
    return (k_low, k_band)


def solution(mesh):
    placed = (
        P(),
        P(),
        P(None, "band", None, None),
        P(None, "band", None, None),
        P(),
        P(),
        P(),
        P(),
        P(),
        P(),
        P("band", None),
        P("band", None),
        P("band", None),
        P("band", None),
    )
    return jax.shard_map(
        shards,
        mesh=mesh,
        in_specs=placed,
        out_specs=(P(), P(None, "band", None, None)),
        check_vma=False,
    )
```

```python
import functools
import math

import jax
import jax.numpy as jnp
from jax import lax
from jax.experimental import pallas as pl
from jax.experimental.pallas import tpu as pltpu
from jax.sharding import PartitionSpec as P


EXPS = 3
OUTER = 4
BLOCKS = (4, 6, 6)
section_weight = 0.2
VMEM_LIMIT = 60 * 1024 * 1024

vmem = pl.BlockSpec(memory_space=pltpu.VMEM)
smem = pl.BlockSpec(memory_space=pltpu.SMEM)
hbm = pl.BlockSpec(memory_space=pl.ANY)


def fill_masks(row_ref, diff_ref, sum_ref=None, start=0):
    sites, height, size = diff_ref.shape
    site_b = jnp.broadcast_to(row_ref[...].astype(jnp.float32), (size, size))
    site_a = jnp.transpose(site_b)[start : start + height]
    site_b = site_b[start : start + height]

    def one_site(s, carry):
        s_f = lax.convert_element_type(s, jnp.float32)
        va = jnp.where(site_a == s_f, 1.0, 0.0)
        vb = jnp.where(site_b == s_f, 1.0, 0.0)
        diff_ref[s] = va - vb
        if sum_ref is not None:
            sum_ref[s] = va + vb
        return carry

    lax.fori_loop(0, sites, one_site, 0)


def split(x):
    high = x.astype(jnp.bfloat16)
    return high, (x - high.astype(jnp.float32)).astype(jnp.bfloat16)


def matmul(x, y):
    def dot(a, b):
        return jnp.dot(a, b, preferred_element_type=jnp.float32)

    return dot(x[0], y[0]) + (dot(x[0], y[1]) + dot(x[1], y[0]))


def commutator(h_re, h_im, y_pair):
    size = y_pair.shape[-1]
    left, right = [], []
    for re, im in zip(h_re, h_im):
        top = jnp.concatenate([re, -im], axis=1)
        low = jnp.concatenate([im, re], axis=1)
        left.append(jnp.concatenate([top, low], axis=0))
        top = jnp.concatenate([re, im], axis=1)
        low = jnp.concatenate([-im, re], axis=1)
        right.append(jnp.concatenate([top, low], axis=0))
    lhs = matmul(left, split(y_pair.reshape(2 * size, size)))
    rhs = matmul(split(jnp.concatenate([y_pair[0], y_pair[1]], axis=1)), right)
    return lhs[:size] - rhs[:, :size], lhs[size:] - rhs[:, size:]


LOW_J, LOW_S, NEAR_M, _, FAR_M, _, COUNTS, OWN_I = range(8)
LOW_A, NEAR_A, _, FAR_A, _, DAMP, OWN_F = range(7)


def prep_kernel(
    low_count, own, src, mode, direction, occ, mag, cos, sin, rate, low_mode, ints, flts
):
    rows, width = src.shape
    modes = occ.shape[1]
    others = low_mode.shape[1]
    own_index, band_size, inner = own[0], own[1], own[2]
    outer = band_size // inner
    f32, i32 = jnp.float32, jnp.int32
    lane_mode = lax.broadcasted_iota(i32, (rows, modes), 1)
    lane_low = lax.broadcasted_iota(i32, (rows, others), 1)
    lane_col = lax.broadcasted_iota(i32, (rows, width), 1)
    occ_f = occ[...].astype(f32)
    mag_b = jnp.broadcast_to(mag[...], (rows, modes))
    cos_b = jnp.broadcast_to(cos[...], (rows, modes))
    sin_b = jnp.broadcast_to(sin[...], (rows, modes))
    rate_b = jnp.broadcast_to(rate[...], (rows, modes))
    mark_b = jnp.broadcast_to(low_mode[...].astype(f32) + 1.0, (rows, others))

    def total(x):
        return jnp.sum(x, axis=1, keepdims=True)

    zero_i = jnp.zeros((rows, width), i32)
    zero_f = jnp.zeros((rows, width), f32)
    int_out = [zero_i] * 6
    flt_out = [zero_f] * 5
    fill = [jnp.zeros((rows, 1), i32)] * 3
    for c in range(width):
        src_c, mode_c = src[:, c : c + 1], mode[:, c : c + 1]
        down = direction[:, c : c + 1] == 1
        hit = lane_mode == mode_c
        level = total(jnp.where(hit, occ_f, 0.0))
        strength = total(jnp.where(hit, mag_b, 0.0))
        amp_down = jnp.sqrt(level * strength)
        amp_up = jnp.sqrt((level + 1.0) * strength)
        alpha = jnp.where(down, amp_down * total(jnp.where(hit, cos_b, 0.0)), amp_up)
        beta = jnp.where(down, amp_down * total(jnp.where(hit, sin_b, 0.0)), 0.0)
        mark = total(jnp.where(lane_low == src_c - 1, mark_b, 0.0))
        held = jnp.where(mark == mode_c.astype(f32) + 1.0, 2.0, 1.0)
        alpha_low = jnp.sqrt(held * strength)
        site = mode_c // EXPS
        live = src_c >= 0
        is_low = live & (src_c < low_count)
        shifted = jnp.maximum(src_c - low_count, 0)
        owner = shifted // rows
        local = is_low | (live & (owner == own_index))
        far_m = (owner % inner) * outer + ((owner // inner) ^ (own_index // inner))
        near_m = jnp.where(is_low, src_c, low_count + shifted % rows)
        lists = (
            (is_low, (src_c, site), (alpha_low,)),
            (local, (near_m, site), (alpha, beta)),
            (live & ~local, (far_m, site), (alpha, beta)),
        )
        at_f = 0
        for which, (flag, int_cols, flt_cols) in enumerate(lists):
            put = (lane_col == fill[which]) & flag
            for i, value in enumerate(int_cols):
                int_out[2 * which + i] = int_out[2 * which + i] + jnp.where(put, value, 0)
            for value in flt_cols:
                flt_out[at_f] = flt_out[at_f] + jnp.where(put, value, 0.0)
                at_f += 1
            fill[which] = fill[which] + jnp.where(flag, 1, 0)
    for i in range(6):
        ints[i] = int_out[i]
    for i in range(5):
        flts[i] = flt_out[i]
    ints[COUNTS] = jnp.where(
        lane_col == 0, fill[0], jnp.where(lane_col == 1, fill[1], fill[2])
    )
    flts[DAMP] = jnp.broadcast_to(total(occ_f * rate_b), (rows, width))
    turn = lax.broadcasted_iota(i32, (rows, 1), 0)
    op = own_index + band_size * turn
    here = jnp.where(op < low_count, 1, 0)
    op = jnp.minimum(op, low_count - 1)
    op_mode = total(jnp.where(lane_low == jnp.maximum(op - 1, 0), mark_b, 0.0)) - 1.0
    op_mode = op_mode.astype(i32)
    hit = lane_mode == op_mode
    raised = jnp.where(op >= 1, 1.0, 0.0)
    amp = jnp.sqrt(total(jnp.where(hit, mag_b, 0.0))) * raised
    amp_cos = amp * total(jnp.where(hit, cos_b, 0.0))
    amp_sin = amp * total(jnp.where(hit, sin_b, 0.0))
    damp = total(jnp.where(hit, rate_b, 0.0)) * raised
    ints[OWN_I] = jnp.where(lane_col == 0, here, jnp.where(lane_col == 1, op_mode // EXPS, op))
    flts[OWN_F] = jnp.where(
        lane_col == 0,
        damp,
        jnp.where(lane_col == 1, amp, jnp.where(lane_col == 2, amp_cos, amp_sin)),
    )


def advance_kernel(rho, kprev, out):
    def advance(i, carry):
        for part in range(2):
            out[i, part] = rho[part, i] + section_weight * kprev[part, i]
        return carry

    lax.fori_loop(0, rho.shape[1], advance, 0)


def send_kernel(first_row, blocks, own, asked, y_band, *rest):
    *outs, held, sems, load_sem = rest
    rows = pl.ds(first_row, held.shape[2])
    load = pltpu.make_async_copy(y_band.at[:, :, rows], held, load_sem.at[0])
    load.start()
    load.wait()

    def copies(i, act):
        out_at = 0
        for at, (start, height, steps, inner) in enumerate(blocks):
            place = own[0] // inner
            many = len(outs[out_at].shape) == 4
            for step in range(steps):
                out = outs[out_at + step] if many else outs[out_at].at[:, step]

                def one(p, carry):
                    entry = asked[(place ^ step) * inner + p, 0, 0] if i == 0 else 0
                    act(
                        pltpu.make_async_copy(
                            held.at[entry, :, pl.ds(start, height)],
                            out.at[p],
                            sems.at[at, step * inner + p],
                        )
                    )
                    return carry

                lax.fori_loop(0, inner, one, 0)
            out_at += steps if many else 1

    copies(0, lambda copy: copy.start())
    copies(1, lambda copy: copy.wait())


def low_kernel(
    mine, ints, flts, y_band, rho_own, kprev_own, rho_top, kprev_top, ham, row, keep, give, out, diff, sems
):
    size = out.shape[-1]
    step = pl.program_id(0)
    half = size // 2

    @pl.when(step == 0)
    def _():
        fill_masks(row, diff)

        def clear(j, carry):
            out[0, j] = jnp.zeros((size, size), jnp.float32)
            out[1, j] = jnp.zeros((size, size), jnp.float32)
            return carry

        lax.fori_loop(0, out.shape[1], clear, 0)

        def operator(n, carry):
            def term(c, inner):
                j, s, amp = ints[LOW_J, n, c], ints[LOW_S, n, c], flts[LOW_A, n, c]
                for part in range(2):
                    rows = pl.ds(part * half, half)
                    weight = amp * diff[s, rows]
                    out[0, j, rows] += weight * y_band[n, 1, rows]
                    out[1, j, rows] -= weight * y_band[n, 0, rows]
                return inner

            return lax.fori_loop(0, ints[COUNTS, n, 0], term, carry)

        lax.fori_loop(0, y_band.shape[0], operator, 0)

    @pl.when(ints[OWN_I, step, 0] == 1)
    def _():
        s, j = ints[OWN_I, step, 1], ints[OWN_I, step, 2]
        damping, amp, amp_cos, amp_sin = (flts[OWN_F, step, i] for i in range(4))
        own = rho_own[:, 0] + section_weight * kprev_own[:, 0]
        real, imag = commutator(split(ham[0]), split(ham[1]), own)
        top = rho_top[:, 0] + section_weight * kprev_top[:, 0]
        site_b = jnp.broadcast_to(row[...].astype(jnp.float32), (size, size))
        s_f = lax.convert_element_type(s, jnp.float32)
        va = jnp.where(jnp.transpose(site_b) == s_f, 1.0, 0.0)
        vb = jnp.where(site_b == s_f, 1.0, 0.0)
        w_re, w_im = amp_cos * (va - vb), amp_sin * (va + vb)
        out[0, j] += imag - damping * own[0] + (w_re * top[1] + w_im * top[0])
        out[1, j] += -real - damping * own[1] + (w_im * top[1] - w_re * top[0])
        up = amp * (va - vb)
        out[0, 0] += up * own[1]
        out[1, 0] -= up * own[0]

    @pl.when(step == pl.num_programs(0) - 1)
    def _():
        count = keep.shape[1]
        copies = [
            pltpu.make_async_copy(out.at[:, pl.ds(place * count, count)], to, sems.at[i])
            for i, (place, to) in enumerate(((mine[0], keep), (1 - mine[0], give)))
        ]
        for copy in copies:
            copy.start()
        for copy in copies:
            copy.wait()


def add_terms(n, width, rows, which, ints, flts, fetch, diff, summ, start):
    count_at, source_at, alpha_at = which
    together = math.gcd(width, 8)
    at = n * width

    def terms(g, state):
        re, im = state
        for u in range(together):
            c = at + g * together + u
            m, s = ints[source_at, c], ints[source_at + 1, c]
            w_re = flts[alpha_at, c] * diff[s, rows]
            w_im = flts[alpha_at + 1, c] * summ[s, rows]
            y_re, y_im = fetch(m, rows)
            re = re + (w_re * y_im + w_im * y_re)
            im = im + (w_im * y_im - w_re * y_re)
        return re, im

    groups = (ints[COUNTS, at + count_at] + (together - 1)) // together
    return lax.fori_loop(0, groups, terms, start)


def own_kernel(flts, y_band, ham, out):
    h_re, h_im = split(ham[0]), split(ham[1])

    def operator(n, carry):
        y_pair = y_band[n]
        damping = flts[DAMP, n, 0]
        real, imag = commutator(h_re, h_im, y_pair)
        out[0, n] = imag - damping * y_pair[0]
        out[1, n] = -real - damping * y_pair[1]
        return carry

    lax.fori_loop(0, y_band.shape[0], operator, 0)


def near_kernel(ints, flts, y_band, rho_low, kprev_low, base, row, out, pool, diff, summ):
    size = out.shape[-1]
    low_count, band_count = rho_low.shape[1], y_band.shape[0]
    parts = 2
    fill_masks(row, diff, summ)

    def advance(i, carry):
        for part in range(2):
            pool[i, part] = rho_low[part, i] + section_weight * kprev_low[part, i]
        return carry

    lax.fori_loop(0, low_count, advance, 0)

    def keep(i, carry):
        pool[low_count + i] = y_band[i]
        return carry

    lax.fori_loop(0, band_count, keep, 0)

    def operator(n, carry):
        for part in range(parts):
            rows = pl.ds(part * (size // parts), size // parts)
            re, im = add_terms(
                n,
                ints.shape[1] // band_count,
                rows,
                (1, NEAR_M, NEAR_A),
                ints,
                flts,
                lambda m, r: (pool[m, 0, r], pool[m, 1, r]),
                diff,
                summ,
                (base[0, n, rows], base[1, n, rows]),
            )
            out[0, n, rows] = re
            out[1, n, rows] = im
        return carry

    lax.fori_loop(0, band_count, operator, 0)


def far_kernel(start, lay, ints, flts, base, row, *rest):
    if lay:
        places, *rest = rest
        pieces, rest = rest[:lay], rest[lay:]
        *rest, lay_out, held, received, diff, summ, sems, laid, in_sems, out_sems = rest
        *parts, out = rest
        pulls = [
            pltpu.make_async_copy(piece, laid.at[i], in_sems.at[i])
            for i, piece in enumerate(pieces)
        ]
        pushes = lay_copies(places, laid, lay_out, out_sems)
    else:
        *parts, out, held, received, diff, summ, sems = rest
        pulls, pushes = [], []
    block = held.shape[2]
    here = pl.ds(start, block)
    loads = [pltpu.make_async_copy(base.at[:, :, here], held, sems.at[0])]
    if len(parts) == 1:
        loads.append(pltpu.make_async_copy(parts[0], received, sems.at[1]))
    else:
        for step, part in enumerate(parts):
            source = part if step else part.at[:, 0]
            loads.append(pltpu.make_async_copy(source, received.at[:, step], sems.at[1 + step]))
    for load in pulls + loads:
        load.start()
    fill_masks(row, diff, summ, start)
    for pull, push in zip(pulls, pushes):
        pull.wait()
        push.start()
    for load in loads:
        load.wait()
    rows = pl.ds(0, block)
    last = received.shape[1] - 1
    shift = last.bit_length()

    def operator(n, carry):
        re, im = add_terms(
            n,
            ints.shape[1] // held.shape[1],
            rows,
            (2, FAR_M, FAR_A),
            ints,
            flts,
            lambda m, r: (received[m >> shift, m & last, 0], received[m >> shift, m & last, 1]),
            diff,
            summ,
            (held[0, n], held[1, n]),
        )
        held[0, n] = re
        held[1, n] = im
        return carry

    lax.fori_loop(0, held.shape[1], operator, 0)
    store = pltpu.make_async_copy(held, out.at[:, :, here], sems.at[0])
    store.start()
    for push in pushes:
        push.wait()
    store.wait()


def part_of(x, index, parts, axis):
    step = x.shape[axis] // parts
    return lax.dynamic_slice_in_dim(x, index * step, step, axis)


def join(pieces, indices, axis):
    if len(pieces) == 2:
        first, second = pieces
        return jnp.where(
            indices[0] == 0,
            jnp.concatenate([first, second], axis=axis),
            jnp.concatenate([second, first], axis=axis),
        )
    shape = list(pieces[0].shape)
    step = shape[axis]
    shape[axis] *= len(pieces)
    out = jnp.zeros(shape, pieces[0].dtype)
    for piece, index in zip(pieces, indices):
        out = lax.dynamic_update_slice_in_dim(out, piece, index * step, axis)
    return out


def lay_copies(places, pieces, out, sems):
    count = pieces.shape[1]
    copies = []
    for i in range(pieces.shape[0]):
        core, axis, stream = i // 4, (i // 2) % 2, i % 2
        half = places[0] if core == 0 else 1 - places[0]
        quarter = places[1 + stream] if axis == 0 else 1 - places[1 + stream]
        start = pl.multiple_of((2 * half + quarter) * count, count)
        copies.append(
            pltpu.make_async_copy(pieces.at[i], out.at[stream, pl.ds(start, count)], sems.at[i])
        )
    return copies


def sum_over_band(keep, give, band_size, outer, own_index):
    inner = band_size // outer
    bits = inner.bit_length() - 1
    place = own_index // inner
    flag = [(own_index >> b) & 1 for b in range(bits)]
    plain = list(range(1, bits))
    orders = (plain, plain[:2][::-1] + plain[2:])

    def swap(value, distance):
        pairs = [(i, i ^ distance) for i in range(band_size)]
        return lax.ppermute(value, "band", pairs)

    x = keep + swap(give, 1)
    streams = [x[0], x[1]]
    for level in range(bits - 1):
        use = [order[level] for order in orders]
        got = [swap(part_of(v, 1 - flag[b], 2, 0), 1 << b) for v, b in zip(streams, use)]
        streams = [part_of(v, flag[b], 2, 0) + g for v, b, g in zip(streams, use, got)]
    x = jnp.stack(streams)
    got = [swap(part_of(x, place ^ d, outer, 1), d * inner) for d in range(1, outer)]
    x = part_of(x, place, outer, 1)
    for other in got:
        x = x + other
    got = [swap(x, d * inner) for d in range(1, outer)]
    x = join([x] + got, [place ^ d for d in range(outer)], 1)
    streams = [x[0], x[1]]
    for level in reversed(range(1, bits - 1)):
        use = [order[level] for order in orders]
        got = [swap(v, 1 << b) for v, b in zip(streams, use)]
        streams = [
            join([v, g], [flag[b], 1 - flag[b]], 0) for v, b, g in zip(streams, use, got)
        ]
    use = [order[0] for order in orders]
    got = [swap(v, 1 << b) for v, b in zip(streams, use)]
    pieces = streams + got
    pieces += [swap(piece, 1) for piece in pieces]
    places = jnp.stack([flag[0]] + [flag[b] for b in use]).astype(jnp.int32)
    return places, pieces


def shards(
    rho_low,
    kprev_low,
    rho_band,
    kprev_band,
    hamiltonian,
    state_site,
    coupling_mag,
    coupling_phase,
    damping_rate,
    low_mode,
    occupation,
    couple_src,
    couple_mode,
    couple_dir,
):
    band_size = lax.axis_size("band")
    own_index = lax.axis_index("band")
    low_count = rho_low.shape[1]
    band_count = rho_band.shape[1]
    size = rho_band.shape[-1]
    sites = coupling_mag.shape[0] // EXPS
    f32 = jnp.float32
    params = functools.partial(pltpu.CompilerParams, vmem_limit_bytes=VMEM_LIMIT)

    shifted = couple_src - low_count
    owner = jnp.where(couple_src >= low_count, shifted // band_count, own_index)
    slot = jnp.where(owner != own_index, shifted % band_count, 0)
    asks = owner[None] == jnp.arange(band_size)[:, None, None]
    wanted = jnp.max(jnp.where(asks, slot[None], 0), axis=(1, 2))
    wanted = jnp.broadcast_to(wanted[:, None, None], (band_size, 1, 128))
    asked = lax.all_to_all(wanted, "band", split_axis=0, concat_axis=0, tiled=True)

    outer = OUTER if band_size % OUTER == 0 else 1
    inner = band_size // outer
    own = jnp.stack([own_index, jnp.int32(band_size), jnp.int32(inner)]).astype(jnp.int32)
    heights = [size * part // sum(BLOCKS) for part in BLOCKS]
    starts = [sum(heights[:i]) for i in range(len(heights))]
    y_band = pl.pallas_call(
        advance_kernel,
        in_specs=[vmem, vmem],
        out_specs=vmem,
        out_shape=jax.ShapeDtypeStruct((band_count, 2, size, size), f32),
        compiler_params=params(),
        name="advance",
    )(rho_band, kprev_band)
    last = len(starts) - 1
    send = []
    for which in (slice(0, 1), slice(1, None)):
        first_row, last_row = starts[which][0], starts[which][-1] + heights[which][-1]
        shapes = []
        for height in heights[which][: None if which.start == 0 else -1]:
            shapes += [(inner, 2, height, size)] * outer
        if which.start:
            shapes.append((inner, outer, 2, heights[last], size))
        send += pl.pallas_call(
            functools.partial(
                send_kernel,
                first_row,
                [(s - first_row, h, outer, inner) for s, h in zip(starts[which], heights[which])],
            ),
            in_specs=[smem, smem, hbm],
            out_specs=[hbm] * len(shapes),
            out_shape=[jax.ShapeDtypeStruct(shape, f32) for shape in shapes],
            scratch_shapes=[
                pltpu.VMEM((band_count, 2, last_row - first_row, size), f32),
                pltpu.SemaphoreType.DMA((len(starts[which]), band_size)),
                pltpu.SemaphoreType.DMA((1,)),
            ],
            compiler_params=params(),
        )(own, asked, y_band)

    groups = [[o * inner + p for p in range(inner)] for o in range(outer)]

    def go_out(value, step):
        pairs = [(i, i ^ (step * inner)) for i in range(band_size)]
        return lax.ppermute(value, "band", pairs)

    def go_in(value):
        return lax.all_to_all(
            value, "band", split_axis=0, concat_axis=0, tiled=True, axis_index_groups=groups
        )

    received = []
    for block in range(last):
        first = send[block * outer : (block + 1) * outer]
        moved = [first[0]] + [go_out(first[step], step) for step in range(1, outer)]
        received.append([go_in(jnp.stack(moved, axis=1))])
    first = go_in(send[-1])
    received.append([first] + [go_out(first[:, step], step) for step in range(1, outer)])

    whole_row = (1, -1)
    ints, flts = pl.pallas_call(
        functools.partial(prep_kernel, low_count),
        in_specs=[smem] + [vmem] * 9,
        out_specs=[vmem, vmem],
        out_shape=[
            jax.ShapeDtypeStruct((8,) + couple_src.shape, jnp.int32),
            jax.ShapeDtypeStruct((7,) + couple_src.shape, f32),
        ],
        name="prep",
    )(
        own,
        couple_src,
        couple_mode,
        couple_dir,
        occupation,
        coupling_mag.reshape(whole_row),
        jnp.cos(coupling_phase).reshape(whole_row),
        jnp.sin(coupling_phase).reshape(whole_row),
        damping_rate.reshape(whole_row),
        low_mode.reshape(whole_row),
    )

    row = state_site[None, :]

    ints_flat, flts_flat = ints.reshape(8, -1), flts.reshape(7, -1)

    turns = -(-low_count // band_size)
    own_op = jnp.minimum(
        own_index + band_size * jnp.arange(turns, dtype=jnp.int32), low_count - 1
    )
    own_block = pl.BlockSpec((2, 1, size, size), lambda g, ops: (0, ops[g], 0, 0))
    top_block = pl.BlockSpec((2, 1, size, size), lambda g, ops: (0, 0, 0, 0))
    half_shape = (2, low_count // 2, size, size)
    keep, give = pl.pallas_call(
        lambda ops, *refs: low_kernel(*refs),
        grid_spec=pltpu.PrefetchScalarGridSpec(
            num_scalar_prefetch=1,
            grid=(turns,),
            in_specs=[smem] * 3
            + [vmem, own_block, own_block, top_block, top_block]
            + [vmem] * 2,
            out_specs=[hbm] * 2,
            scratch_shapes=[
                pltpu.VMEM((2, low_count, size, size), f32),
                pltpu.VMEM((sites, size, size), f32),
                pltpu.SemaphoreType.DMA((2,)),
            ],
        ),
        out_shape=[jax.ShapeDtypeStruct(half_shape, f32)] * 2,
        compiler_params=params(),
        name="low",
    )(
        own_op,
        (own_index & 1).astype(jnp.int32)[None],
        ints,
        flts,
        y_band,
        rho_low,
        kprev_low,
        rho_low,
        kprev_low,
        hamiltonian,
        row,
    )
    flat = (2, -1, size)
    places, pieces = sum_over_band(
        keep.reshape(flat), give.reshape(flat), band_size, outer, own_index
    )

    base = pl.pallas_call(
        own_kernel,
        in_specs=[smem] + [vmem] * 2,
        out_specs=vmem,
        out_shape=jax.ShapeDtypeStruct((2, band_count, size, size), f32),
        compiler_params=params(),
        name="own",
    )(flts, y_band, hamiltonian)

    def far_terms(k_band, block, pieces=()):
        height = heights[block]
        parts = received[block]
        out_specs, out_shape = hbm, jax.ShapeDtypeStruct((2, band_count, size, size), f32)
        scratch = [
            pltpu.VMEM((2, band_count, height, size), f32),
            pltpu.VMEM((inner, outer, 2, height, size), f32),
            pltpu.VMEM((sites, height, size), f32),
            pltpu.VMEM((sites, height, size), f32),
            pltpu.SemaphoreType.DMA((1 + len(parts),)),
        ]
        lay = []
        if pieces:
            lay = [places, *pieces]
            out_specs = [hbm, hbm]
            out_shape = [out_shape, jax.ShapeDtypeStruct((2, low_count * size, size), f32)]
            scratch.append(pltpu.VMEM((len(pieces),) + pieces[0].shape, f32))
            scratch += [pltpu.SemaphoreType.DMA((len(pieces),))] * 2
        return pl.pallas_call(
            functools.partial(far_kernel, starts[block], len(pieces)),
            in_specs=[smem] * 2
            + [hbm, vmem]
            + ([smem] + [hbm] * len(pieces) if pieces else [])
            + [hbm] * len(parts),
            out_specs=out_specs,
            out_shape=out_shape,
            scratch_shapes=scratch,
            input_output_aliases={2: 0},
            compiler_params=params(),
        )(ints_flat, flts_flat, k_band, row, *lay, *parts)

    k_band = base
    for block in range(last):
        k_band = far_terms(k_band, block)
    k_band = pl.pallas_call(
        near_kernel,
        in_specs=[smem] * 2 + [vmem] * 5,
        out_specs=vmem,
        out_shape=jax.ShapeDtypeStruct((2, band_count, size, size), f32),
        scratch_shapes=[pltpu.VMEM((low_count + band_count, 2, size, size), f32)]
        + [pltpu.VMEM((sites, size, size), f32)] * 2,
        compiler_params=params(),
        name="near",
    )(ints_flat, flts_flat, y_band, rho_low, kprev_low, k_band, row)
    k_band, k_low = far_terms(k_band, last, pieces)
    k_low = k_low.reshape(rho_low.shape)
    return (k_low, k_band)


def solution(mesh):
    placed = (
        P(),
        P(),
        P(None, "band", None, None),
        P(None, "band", None, None),
        P(),
        P(),
        P(),
        P(),
        P(),
        P(),
        P("band", None),
        P("band", None),
        P("band", None),
        P("band", None),
    )
    return jax.shard_map(
        shards,
        mesh=mesh,
        in_specs=placed,
        out_specs=(P(), P(None, "band", None, None)),
        check_vma=False,
    )
```
